128 devices in a mesh: row: 8 (over z, core), col: 16 (over y, x).
Axes of the slice: x: 4, y: 4, z: 4, core: 2. Of those that a mesh axis runs over, the one named last changes fastest.
Arguments:
- front_diag: float32 [1024, 1024], replicated, may hold values from -4 to 16, as said below
- panel_rows: float32 [16384, 1024], P(('row', 'col')), may hold values from -1.2 to 1.2
- trailing: float32 [16384, 16384], P('row', 'col'), may hold values from -6 to 6
- pattern: int32 [64, 64], P('row', 'col'), may hold values 0 or 1
Outputs:
- diag_factor: float32 [1024, 1024], replicated
- panel_factor: float32 [16384, 1024], P(('row', 'col'))
- schur: float32 [16384, 16384], P('row', 'col')
The draws below stay inside these ranges and needn't reach their ends.
Inputs may be any that keep to these rules, and one draw needn't show every extreme that they name: front_diag is symmetric and positive definite, with smallest eigenvalue at least 0.5.
All inputs are finite; a program needn't handle non-finite values. No bound on the sum of `pattern` on one device may be relied on, other than what follows from the above.
Results may differ from the reference program's by a relative error of at most 0.0003.
Values sent between devices are 32-bit elements; how exact they have to be, the bound alone decides.
A program may use at most 128 MiB of HBM per device.

```python
import jax
import jax.numpy as jnp
from jax import lax

W = 512
BLOCK = 256
TRAIL = 16384
PANEL = 1024
NB = 64


def draw_front_diag(key, part):
    order = 2 * W
    first = jax.random.fold_in(key, 11)
    factor = jax.random.normal(first, (order, order), jnp.float32)
    gram = jnp.dot(factor, factor.T, precision=lax.Precision.HIGHEST) / order
    gram = 0.5 * (gram + gram.T)
    ident = jnp.eye(order, dtype=jnp.float32)
    return gram + 0.5 * ident


def set_ends(array, key, low, high):
    longest = array.shape.index(max(array.shape))
    spots = []
    for shift in (0, 1):
        where = [jax.random.randint(jax.random.fold_in(key, axis), (), 0, length) for axis, length in enumerate(array.shape)]
        where[longest] = (where[longest] + shift) % array.shape[longest]
        spots.append(tuple(where))
    return array.at[spots[0]].set(low).at[spots[1]].set(high)


def block_scale(key, extent, pieces, least, top_value):
    gain, own = 1.0, jax.random.fold_in(key, 6)
    for dim, blocks in pieces:
        steps = jnp.exp(jax.random.uniform(jax.random.fold_in(own, dim), (blocks,), jnp.float32, least / len(pieces), top_value / len(pieces)))
        gain = gain * jnp.repeat(steps, extent[dim] // blocks).reshape([-1 if axis == dim else 1 for axis in range(len(extent))])
    return gain


def centred(rng, extent, spread, most, shards=(), kind=jnp.bfloat16):
    level = block_scale(rng, extent, shards, -0.22, 0.18) if shards else 1.0
    result = jax.random.normal(rng, extent, jnp.float32) * spread * level
    return jnp.minimum(jnp.maximum(result, -most), most).astype(kind)


def setup_inputs(seed: int = 0) -> dict:
    streams_of = jax.random.split(jax.random.key(seed), 5)
    front_diag = draw_front_diag(jax.random.fold_in(streams_of[4], 71), 0)
    panel_rows = centred(streams_of[1], (TRAIL, PANEL), 0.2, 1.2, ((0, 128),), jnp.float32)
    trailing = centred(streams_of[2], (TRAIL, TRAIL), 1.0, 6.0, ((0, 8), (1, 16)), jnp.float32)
    pattern = set_ends((jax.random.randint(streams_of[3], (NB, NB), 0, 2) < 1).astype(jnp.int32), jax.random.fold_in(streams_of[3], 1), 0, 1)
    return dict(front_diag=front_diag, panel_rows=panel_rows, trailing=trailing, pattern=pattern)


def reference(front_diag, panel_rows, trailing, pattern):
    diag_factor = jnp.linalg.cholesky(front_diag)
    panel_factor = jax.scipy.linalg.solve_triangular(diag_factor, panel_rows.T, lower=True).T
    blocks = jnp.arange(NB)
    keep = pattern.astype(jnp.float32) * (blocks[:, None] >= blocks[None, :]).astype(jnp.float32)
    column_keep = jnp.repeat(keep, BLOCK, axis=1)

    def one_row(index):
        start = (index * BLOCK).astype(jnp.int32)
        rows = lax.dynamic_slice_in_dim(panel_factor, start, BLOCK, 0)
        update = jnp.dot(rows, panel_factor.T, precision=lax.Precision.HIGHEST)
        old = lax.dynamic_slice_in_dim(trailing, start, BLOCK, 0)
        return old - update * column_keep[index][None, :]
    schur = lax.map(one_row, jnp.arange(NB).astype(jnp.int32)).reshape(TRAIL, TRAIL)
    return (diag_factor, panel_factor, schur)
```

```python
import jax
import jax.numpy as jnp
from jax import lax
from jax.experimental import pallas as pl
from jax.experimental.pallas import tpu as pltpu
from jax.sharding import PartitionSpec as P

BLOCK = 256
HI = lax.Precision.HIGHEST


def factor_tile(s, t):
    sub = lax.broadcasted_iota(jnp.int32, (8, 128), 0)
    def wide(x, c):
        return jnp.broadcast_to(x[:, c:c + 1], (8, 128))
    def tall(x, k):
        return jnp.broadcast_to(x[k:k + 1, :], (8, 128))
    n = len(s)
    for g in range(n):
        r, q = s[g], t[g]
        c = [wide(r, 8 * g + m) for m in range(8)]
        u = jnp.zeros((8, 128), jnp.float32)
        w = u
        for k in range(8):
            here = sub == k
            f = c[k]
            p = tall(f, k)
            inv = 1.0 / p
            root = lax.rsqrt(p)
            rk, qk = tall(r, k), tall(q, k)
            u = jnp.where(here, rk * root, u)
            w = jnp.where(here, qk * root, w)
            r = jnp.where(here, rk * inv, r - (f * rk) * inv)
            q = jnp.where(here, qk * inv, q - (f * qk) * inv)
            for m in range(k + 1, 8):
                cm = tall(c[m], k)
                c[m] = jnp.where(here, cm * inv, c[m] - (f * cm) * inv)
        for h in range(g + 1, n):
            sh, th = s[h], t[h]
            ds, dt = None, None
            for m in range(8):
                b = wide(s[h], 8 * g + m)
                a1, a2 = b * tall(r, m), b * tall(q, m)
                ds = a1 if ds is None else ds + a1
                dt = a2 if dt is None else dt + a2
            s[h], t[h] = sh - ds, th - dt
        s[g], t[g] = u, w
    return s, t

def chol_kernel(a_ref, l_ref, w_ref, g_ref, u_ref, wd_ref):
    n = a_ref.shape[0]
    nb = n // 128
    w_ref[...] = a_ref[...]
    l_ref[...] = jnp.zeros_like(l_ref)
    sub = lax.broadcasted_iota(jnp.int32, (8, 128), 0)
    lane = lax.broadcasted_iota(jnp.int32, (8, 128), 1)
    lane_all = lax.broadcasted_iota(jnp.int32, (128, n), 1)

    def panel(p, carry):
        o = pl.multiple_of(p * 128, 128)
        s = [w_ref[pl.ds(o + 8 * g, 8), pl.ds(o, 128)] for g in range(16)]
        t = [(lane == sub + 8 * g).astype(jnp.float32) for g in range(16)]
        s, t = factor_tile(s, t)
        for g in range(16):
            u_ref[8 * g:8 * g + 8, :] = jnp.where(lane >= sub + 8 * g, s[g], 0.0)
            wd_ref[8 * g:8 * g + 8, :] = t[g]
        wd = wd_ref[...]
        rows = w_ref[pl.ds(o, 128), :]
        g_ref[...] = jnp.dot(wd, rows, precision=HI, preferred_element_type=jnp.float32)
        g_ref[:, pl.ds(o, 128)] = wd
        w_ref[pl.ds(o, 128), :] = jnp.where(lane_all < o + 128, g_ref[...], 0.0)
        l_ref[pl.ds(o, 128), pl.ds(o, 128)] = u_ref[...].T

        def below(i, c):
            oi = pl.multiple_of(i * 128, 128)
            li = g_ref[:, pl.ds(oi, 128)].T
            l_ref[pl.ds(oi, 128), pl.ds(o, 128)] = li
            w_ref[pl.ds(oi, 128), pl.ds(o, 128)] = jnp.zeros((128, 128), jnp.float32)
            w_ref[pl.ds(oi, 128), :] -= jnp.dot(li, g_ref[...], precision=HI, preferred_element_type=jnp.float32)
            return c
        lax.fori_loop(p + 1, nb, below, 0)
        return carry
    lax.fori_loop(0, nb, panel, 0)

def chol(a):
    n = a.shape[0]
    f32 = jnp.float32
    return pl.pallas_call(
        chol_kernel,
        out_shape=(jax.ShapeDtypeStruct((n, n), f32),) * 2,
        in_specs=[pl.BlockSpec(memory_space=pltpu.VMEM)],
        out_specs=(pl.BlockSpec(memory_space=pltpu.VMEM),) * 2,
        scratch_shapes=[pltpu.VMEM((128, n), f32), pltpu.VMEM((128, 128), f32), pltpu.VMEM((128, 128), f32)],
        compiler_params=pltpu.CompilerParams(vmem_limit_bytes=60 << 20),
        name="factor",
    )(a)

NT = (((1,), (1,)), ((), ()))
NN = (((1,), (0,)), ((), ()))


def halves(x):
    high = x.astype(jnp.bfloat16)
    return high, (x - high.astype(jnp.float32)).astype(jnp.bfloat16)


def dot3(a, b, dims):
    def one(x, y):
        return lax.dot_general(x, y, dims, preferred_element_type=jnp.float32)
    return one(a[0], b[0]) + (one(a[0], b[1]) + one(a[1], b[0]))


def apply_kernel(w_ref, own_ref, c_ref, x_ref, yh_ref, yl_ref, wh, wl, ch, cl, zh, zl):
    n = w_ref.shape[0]
    wh[...], wl[...] = halves(w_ref[...])
    ch[...], cl[...] = halves(c_ref[...])
    x_ref[...] = lax.dot_general(own_ref[...], w_ref[...], NT, precision=HI, preferred_element_type=jnp.float32)
    for p in range(0, n, BLOCK):
        e = p + BLOCK
        z = dot3((ch[:, :e], cl[:, :e]), (wh[p:e, :e], wl[p:e, :e]), NT)
        zh[:, p:e], zl[:, p:e] = halves(z)
    for p in range(0, n, BLOCK):
        e = p + BLOCK
        y = dot3((zh[:, p:], zl[:, p:]), (wh[p:, p:e], wl[p:, p:e]), NN)
        yh_ref[:, p:e], yl_ref[:, p:e] = halves(y)


def apply_inverse(w, own, c):
    f32, bf = jnp.float32, jnp.bfloat16
    n, m = w.shape[0], c.shape[0]
    vm = pl.BlockSpec(memory_space=pltpu.VMEM)
    return pl.pallas_call(
        apply_kernel,
        out_shape=(jax.ShapeDtypeStruct(own.shape, f32), jax.ShapeDtypeStruct((m, n), bf), jax.ShapeDtypeStruct((m, n), bf)),
        in_specs=[vm] * 3,
        out_specs=(vm,) * 3,
        scratch_shapes=[pltpu.VMEM((n, n), bf)] * 2 + [pltpu.VMEM((m, n), bf)] * 4,
        compiler_params=pltpu.CompilerParams(vmem_limit_bytes=60 << 20),
        name="apply",
    )(w, own, c)


def update_kernel(keep_ref, r_ref, yh_ref, yl_ref, t_ref, o_ref, rh, rl):
    i = pl.program_id(0)
    cols = o_ref.shape[1] // BLOCK
    rh[...], rl[...] = halves(r_ref[...])
    for j in range(cols):
        part = slice(j * BLOCK, (j + 1) * BLOCK)
        kept = keep_ref[i * cols + j] != 0

        @pl.when(kept)
        def _():
            d = dot3((rh[...], rl[...]), (yh_ref[part, :], yl_ref[part, :]), NT)
            o_ref[:, part] = t_ref[:, part] - d

        @pl.when(jnp.logical_not(kept))
        def _():
            o_ref[:, part] = t_ref[:, part]


def update(keep, rows, yh, yl, trailing):
    m, n = trailing.shape
    k = rows.shape[1]
    return pl.pallas_call(
        update_kernel,
        out_shape=jax.ShapeDtypeStruct((m, n), jnp.float32),
        grid_spec=pltpu.PrefetchScalarGridSpec(
            num_scalar_prefetch=1,
            grid=(m // BLOCK,),
            in_specs=[
                pl.BlockSpec((BLOCK, k), lambda i, s: (i, 0)),
                pl.BlockSpec((n, k), lambda i, s: (0, 0)),
                pl.BlockSpec((n, k), lambda i, s: (0, 0)),
                pl.BlockSpec((BLOCK, n), lambda i, s: (i, 0)),
            ],
            out_specs=pl.BlockSpec((BLOCK, n), lambda i, s: (i, 0)),
            scratch_shapes=[pltpu.VMEM((BLOCK, k), jnp.bfloat16)] * 2,
        ),
        compiler_params=pltpu.CompilerParams(vmem_limit_bytes=60 << 20),
        name="update",
    )(keep, rows, yh, yl, trailing)


def local(front_diag, panel_rows, trailing, pattern):
    nrow, ncol = lax.axis_size("row"), lax.axis_size("col")
    ratio = ncol // nrow
    pairs = []
    for c in range(ncol):
        for r in range(nrow):
            pairs.append(((c // ratio) * ncol + (c % ratio) * nrow + r, r * ncol + c))
    rows = lax.all_gather(panel_rows, "col", axis=0, tiled=True)
    piece = lax.ppermute(panel_rows, ("row", "col"), pairs)
    col_rows = lax.all_gather(piece, "row", axis=0, tiled=True)
    diag_factor, inverse = chol(front_diag)
    panel_factor, yh, yl = apply_inverse(inverse, panel_rows, col_rows)
    row_blocks, col_blocks = pattern.shape
    row_index = lax.axis_index("row") * row_blocks + jnp.arange(row_blocks)
    col_index = lax.axis_index("col") * col_blocks + jnp.arange(col_blocks)
    keep = pattern * (row_index[:, None] >= col_index[None, :]).astype(jnp.int32)
    schur = update(keep.reshape(-1), rows, yh, yl, trailing)
    return (diag_factor, panel_factor, schur)


def solution(mesh):
    return jax.shard_map(
        local,
        mesh=mesh,
        in_specs=(P(), P(("row", "col"), None), P("row", "col"), P("row", "col")),
        out_specs=(P(), P(("row", "col"), None), P("row", "col")),
        check_vma=False,
    )
```

```python
import jax
import jax.numpy as jnp
from jax import lax
from jax.experimental import pallas as pl
from jax.experimental.pallas import tpu as pltpu
from jax.sharding import PartitionSpec as P

BLOCK = 256
SIDE = 4
HI = lax.Precision.HIGHEST
MESH = pl.DeviceIdType.MESH

NT = (((1,), (1,)), ((), ()))
NN = (((1,), (0,)), ((), ()))


def halves(x):
    high = x.astype(jnp.bfloat16)
    return high, (x - high.astype(jnp.float32)).astype(jnp.bfloat16)


def dot3(a, b, dims):
    def one(x, y):
        return lax.dot_general(x, y, dims, preferred_element_type=jnp.float32)
    return one(a[0], b[0]) + (one(a[0], b[1]) + one(a[1], b[0]))


def factor_tile(s, t):
    sub = lax.broadcasted_iota(jnp.int32, (8, 128), 0)
    def wide(x, c):
        return jnp.broadcast_to(x[:, c:c + 1], (8, 128))
    def tall(x, k):
        return jnp.broadcast_to(x[k:k + 1, :], (8, 128))
    n = len(s)
    for g in range(n):
        r, q = s[g], t[g]
        c = [wide(r, 8 * g + m) for m in range(8)]
        u = jnp.zeros((8, 128), jnp.float32)
        w = u
        for k in range(8):
            here = sub == k
            f = c[k]
            p = tall(f, k)
            inv = 1.0 / p
            root = lax.rsqrt(p)
            rk, qk = tall(r, k), tall(q, k)
            u = jnp.where(here, rk * root, u)
            w = jnp.where(here, qk * root, w)
            r = jnp.where(here, rk * inv, r - (f * rk) * inv)
            q = jnp.where(here, qk * inv, q - (f * qk) * inv)
            for m in range(k + 1, 8):
                cm = tall(c[m], k)
                c[m] = jnp.where(here, cm * inv, c[m] - (f * cm) * inv)
        for h in range(g + 1, n):
            sh, th = s[h], t[h]
            ds, dt = None, None
            for m in range(8):
                b = wide(s[h], 8 * g + m)
                a1, a2 = b * tall(r, m), b * tall(q, m)
                ds = a1 if ds is None else ds + a1
                dt = a2 if dt is None else dt + a2
            s[h], t[h] = sh - ds, th - dt
        s[g], t[g] = u, w
    return s, t


class Exchange:
    def __init__(self, own, rows, cols, sems):
        self.own, self.rows, self.cols = own, rows, cols
        self.row_send, self.row_recv, self.col_send, self.col_recv, self.pair_send, self.here = sems
        row, col = lax.axis_index("row"), lax.axis_index("col")
        self.z, self.k, self.y, self.x = row // 2, row % 2, col // SIDE, col % SIDE
        self.piece = own.shape[0]
        self.half = self.piece // 2
        self.quarter = self.piece // 4

    def device(self, dx=0, dy=0, dz=0, dk=0):
        z, k = lax.rem(self.z + dz + SIDE, SIDE), lax.rem(self.k + dk, 2)
        y, x = lax.rem(self.y + dy + SIDE, SIDE), lax.rem(self.x + dx + SIDE, SIDE)
        return (z * 2 + k, y * SIDE + x)

    def greet(self):
        near = [self.device(dx=1), self.device(dx=-1), self.device(dy=1), self.device(dy=-1),
                self.device(dz=1), self.device(dz=-1), self.device(dk=1)]
        barrier = pltpu.get_barrier_semaphore()
        for device in near:
            pl.semaphore_signal(barrier, inc=1, device_id=device, device_id_type=MESH)
        pl.semaphore_wait(barrier, len(near))

    def origin(self, h, a, b):
        dx, dy = (a, b) if h == 0 else (b, a)
        return lax.rem(self.x + dx, SIDE), lax.rem(self.y + dy, SIDE)

    def row_slot(self, h, a, b, q=None):
        x, y = self.origin(h, a, b)
        start = (y * SIDE + x) * self.piece + h * self.half
        if q is None:
            return self.rows.at[pl.ds(pl.multiple_of(start, self.quarter), self.half)]
        return self.rows.at[pl.ds(pl.multiple_of(start + q * self.quarter, self.quarter), self.quarter)]

    def own_half(self, h):
        return self.own.at[pl.ds(h * self.half, self.half)]

    def row_copy(self, h, a, b, q, along, sign):
        to_a = (a - sign) % SIDE if along == 0 else a
        to_b = (b - sign) % SIDE if along == 1 else b
        index = ((h * SIDE + to_a) * SIDE + to_b) * 2 + (q or 0)
        slot = self.row_slot(h, a, b, q)
        src = self.own_half(h) if (a, b) == (0, 0) else slot
        on_x = (along == 0) == (h == 0)
        device = self.device(dx=sign) if on_x else self.device(dy=sign)
        return pltpu.make_async_remote_copy(
            src_ref=src, dst_ref=slot, send_sem=self.row_send.at[index], recv_sem=self.row_recv.at[index],
            device_id=device, device_id_type=MESH)

    def row_wait(self, h, a, b, q=None):
        index = ((h * SIDE + a) * SIDE + b) * 2 + (q or 0)
        slot = self.row_slot(h, a, b, q)
        pltpu.make_async_copy(slot, slot, self.row_recv.at[index]).wait()

    def sends(self):
        out = []
        for h in (0, 1):
            for sign in (1, -1):
                out.append((0, h, 0, 0, None, 0, sign))
        for h in (0, 1):
            for sign in (1, -1):
                out.append((0, h, 0, 0, None, 1, sign))
        for h in (0, 1):
            out += [(1, h, 3, 0, 0, 0, 1), (1, h, 1, 0, 1, 0, -1)]
        for h in (0, 1):
            for a in (1, 3):
                for sign in (1, -1):
                    out.append((1, h, a, 0, None, 1, sign))
        for h in (0, 1):
            for sign in (1, -1):
                out.append((2, h, 2, 0, None, 1, sign))
        for wave, places in ((2, (0,)), (3, (1, 3)), (4, (2,))):
            for h in (0, 1):
                for a in places:
                    out += [(wave, h, a, 3, 0, 1, 1), (wave, h, a, 1, 1, 1, -1)]
        return out

    ARRIVALS = (
        (),
        ((1, 0), (3, 0)),
        ((2, 0), (0, 1), (0, 3)),
        ((1, 1), (1, 3), (3, 1), (3, 3)),
        ((2, 1), (2, 3), (0, 2)),
        ((1, 2), (3, 2), (2, 2)),
    )

    def col_slot(self, h, a, b):
        x, y = self.origin(h, a, b)
        start = (lax.rem(y, 2) * SIDE + x) * self.piece + h * self.half
        return self.cols.at[pl.ds(pl.multiple_of(start, self.half), self.half)]

    def col_index(self, h, a, b):
        return (h * SIDE + a) * SIDE + b

    def in_cols(self, h, a, b):
        _, y = self.origin(h, a, b)
        return y // 2 == lax.rem(self.x, 2)

    def holder(self):
        return self.k == self.x // 2

    def hop(self, h):
        return lax.rem(self.z - self.y + SIDE, SIDE) if h == 0 else lax.rem(self.y - self.z + SIDE, SIDE)

    def col_source(self, h, a, b, first):
        if not first:
            return self.col_slot(h, a, b)
        return self.own_half(h) if (a, b) == (0, 0) else self.row_slot(h, a, b)

    def along(self, h, a, b, first):
        index = self.col_index(h, a, b)
        return pltpu.make_async_remote_copy(
            src_ref=self.col_source(h, a, b, first), dst_ref=self.col_slot(h, a, b),
            send_sem=self.col_send.at[index], recv_sem=self.col_recv.at[index],
            device_id=self.device(dz=1 if h == 0 else -1), device_id_type=MESH)

    def across(self, h, a, b, first):
        index = self.col_index(h, a, b)
        return pltpu.make_async_remote_copy(
            src_ref=self.col_source(h, a, b, first), dst_ref=self.col_slot(h, a, b),
            send_sem=self.pair_send.at[index], recv_sem=self.col_recv.at[index],
            device_id=self.device(dk=1), device_id_type=MESH)

    def keep_copy(self, h, a, b):
        src = self.col_source(h, a, b, True)
        return pltpu.make_async_copy(src, self.col_slot(h, a, b), self.here.at[self.col_index(h, a, b)])

    def col_wait(self, h, a, b):
        slot = self.col_slot(h, a, b)
        pltpu.make_async_copy(slot, slot, self.col_recv.at[self.col_index(h, a, b)]).wait()

    def pieces(self, wave):
        return [(h, a, b) for h in (0, 1) for a, b in (((0, 0),) if wave == 0 else self.ARRIVALS[wave])]

    def start_rows(self, wave):
        for h in (0, 1):
            for a, b in self.ARRIVALS[wave]:
                if b == 2 or (a == 2 and b == 0):
                    self.row_wait(h, a, b, 0)
                    self.row_wait(h, a, b, 1)
                else:
                    self.row_wait(h, a, b)
        for entry in self.sends():
            if entry[0] == wave:
                self.row_copy(*entry[1:]).start()

    def start_cols(self, wave):
        for h, a, b in self.pieces(wave):
            @pl.when(self.in_cols(h, a, b) & self.holder() & (self.hop(h) == 0))
            def _():
                self.along(h, a, b, True).start()
                self.across(h, a, b, True).start()
                self.keep_copy(h, a, b).start()

    def relay_cols(self, wave, hop):
        for h, a, b in self.pieces(wave):
            @pl.when(self.in_cols(h, a, b) & self.holder() & (self.hop(h) == hop))
            def _():
                self.col_wait(h, a, b)
                if hop < SIDE - 1:
                    self.along(h, a, b, False).start()
                self.across(h, a, b, False).start()

    def finish_cols(self):
        for wave in range(len(self.ARRIVALS)):
            for h, a, b in self.pieces(wave):
                inside = self.in_cols(h, a, b)

                @pl.when(inside & self.holder() & (self.hop(h) == 0))
                def _():
                    self.keep_copy(h, a, b).wait()

                @pl.when(inside & jnp.logical_not(self.holder()))
                def _():
                    self.col_wait(h, a, b)

    def finish(self):
        for entry in self.sends():
            self.row_copy(*entry[1:]).wait_send()
        for wave in range(len(self.ARRIVALS)):
            for h, a, b in self.pieces(wave):
                @pl.when(self.in_cols(h, a, b) & self.holder())
                def _():
                    self.across(h, a, b, False).wait_send()

                    @pl.when(self.hop(h) < SIDE - 1)
                    def _():
                        self.along(h, a, b, False).wait_send()


ROW_POINTS = (0, 2, 4, 7, 9, 11)
LAG = 1


def transfers(exchange, point):
    for wave, at in enumerate(ROW_POINTS):
        if at == point:
            exchange.start_rows(wave)
            exchange.start_cols(wave)
        for hop in range(1, SIDE):
            if at + LAG * hop == point:
                exchange.relay_cols(wave, hop)


def factor_kernel(a_ref, own_ref, l_ref, x_ref, yh_ref, yl_ref, rows_ref,
                  w_ref, g_ref, u_ref, wd_ref, cols_ref, wh, wl, ch, cl, zh, zl, sem_own, *sems):
    n = a_ref.shape[0]
    nb = n // 128
    exchange = Exchange(own_ref, rows_ref, cols_ref, sems)
    exchange.greet()
    first = pl.multiple_of(lax.axis_index("col") * own_ref.shape[0], own_ref.shape[0])
    keep_own = pltpu.make_async_copy(own_ref, rows_ref.at[pl.ds(first, own_ref.shape[0])], sem_own)
    keep_own.start()
    transfers(exchange, 0)
    w_ref[...] = a_ref[...]
    l_ref[...] = jnp.zeros_like(l_ref)
    sub = lax.broadcasted_iota(jnp.int32, (8, 128), 0)
    lane = lax.broadcasted_iota(jnp.int32, (8, 128), 1)
    lane_all = lax.broadcasted_iota(jnp.int32, (128, n), 1)

    def panel(p, carry):
        o = pl.multiple_of(p * 128, 128)
        s = [w_ref[pl.ds(o + 8 * g, 8), pl.ds(o, 128)] for g in range(16)]
        t = [(lane == sub + 8 * g).astype(jnp.float32) for g in range(16)]
        s, t = factor_tile(s, t)
        for g in range(16):
            u_ref[8 * g:8 * g + 8, :] = jnp.where(lane >= sub + 8 * g, s[g], 0.0)
            wd_ref[8 * g:8 * g + 8, :] = t[g]
        for k in range(nb):
            @pl.when(p == k)
            def _():
                transfers(exchange, 2 * k + 1)
        wd = wd_ref[...]
        rows = w_ref[pl.ds(o, 128), :]
        g_ref[...] = jnp.dot(wd, rows, precision=HI, preferred_element_type=jnp.float32)
        g_ref[:, pl.ds(o, 128)] = wd
        w_ref[pl.ds(o, 128), :] = jnp.where(lane_all < o + 128, g_ref[...], 0.0)
        l_ref[pl.ds(o, 128), pl.ds(o, 128)] = u_ref[...].T

        def below(i, c):
            oi = pl.multiple_of(i * 128, 128)
            li = g_ref[:, pl.ds(oi, 128)].T
            l_ref[pl.ds(oi, 128), pl.ds(o, 128)] = li
            w_ref[pl.ds(oi, 128), pl.ds(o, 128)] = jnp.zeros((128, 128), jnp.float32)
            w_ref[pl.ds(oi, 128), :] -= jnp.dot(li, g_ref[...], precision=HI, preferred_element_type=jnp.float32)
            return c
        lax.fori_loop(p + 1, nb, below, 0)
        for k in range(nb):
            @pl.when(p == k)
            def _():
                transfers(exchange, 2 * k + 2)
        return carry
    lax.fori_loop(0, nb, panel, 0)

    x_ref[...] = lax.dot_general(own_ref[...], w_ref[...], NT, precision=HI, preferred_element_type=jnp.float32)
    wh[...], wl[...] = halves(w_ref[...])
    exchange.finish_cols()
    ch[...], cl[...] = halves(cols_ref[...])
    for p in range(0, n, BLOCK):
        e = p + BLOCK
        z = dot3((ch[:, :e], cl[:, :e]), (wh[p:e, :e], wl[p:e, :e]), NT)
        zh[:, p:e], zl[:, p:e] = halves(z)
    for p in range(0, n, BLOCK):
        e = p + BLOCK
        y = dot3((zh[:, p:], zl[:, p:]), (wh[p:, p:e], wl[p:, p:e]), NN)
        yh_ref[:, p:e], yl_ref[:, p:e] = halves(y)
    exchange.finish()
    keep_own.wait()


def factor(front_diag, own, cols):
    f32, bf = jnp.float32, jnp.bfloat16
    n = front_diag.shape[0]
    pieces = lax.axis_size("col")
    vm, anywhere = pl.BlockSpec(memory_space=pltpu.VMEM), pl.BlockSpec(memory_space=pl.ANY)
    dma = pltpu.SemaphoreType.DMA
    return pl.pallas_call(
        factor_kernel,
        out_shape=(
            jax.ShapeDtypeStruct((n, n), f32),
            jax.ShapeDtypeStruct(own.shape, f32),
            jax.ShapeDtypeStruct((cols, n), bf),
            jax.ShapeDtypeStruct((cols, n), bf),
            jax.ShapeDtypeStruct((pieces * own.shape[0], n), f32),
        ),
        in_specs=[vm, vm],
        out_specs=(vm, vm, vm, vm, anywhere),
        scratch_shapes=[
            pltpu.VMEM((n, n), f32), pltpu.VMEM((128, n), f32), pltpu.VMEM((128, 128), f32), pltpu.VMEM((128, 128), f32),
            pltpu.VMEM((cols, n), f32),
            pltpu.VMEM((n, n), bf), pltpu.VMEM((n, n), bf),
            pltpu.VMEM((cols, n), bf), pltpu.VMEM((cols, n), bf), pltpu.VMEM((cols, n), bf), pltpu.VMEM((cols, n), bf),
            dma, dma((64,)), dma((64,)), dma((32,)), dma((32,)), dma((32,)), dma((32,)),
        ],
        compiler_params=pltpu.CompilerParams(vmem_limit_bytes=60 << 20, collective_id=0, has_side_effects=True),
        name="factor",
    )(front_diag, own)

def update_kernel(keep_ref, r_ref, yh_ref, yl_ref, t_ref, o_ref, rh, rl):
    i = pl.program_id(0)
    cols = o_ref.shape[1] // BLOCK
    rh[...], rl[...] = halves(r_ref[...])
    for j in range(cols):
        part = slice(j * BLOCK, (j + 1) * BLOCK)
        kept = keep_ref[i * cols + j] != 0

        @pl.when(kept)
        def _():
            d = dot3((rh[...], rl[...]), (yh_ref[part, :], yl_ref[part, :]), NT)
            o_ref[:, part] = t_ref[:, part] - d

        @pl.when(jnp.logical_not(kept))
        def _():
            o_ref[:, part] = t_ref[:, part]


def update(keep, rows, yh, yl, trailing):
    m, n = trailing.shape
    k = rows.shape[1]
    return pl.pallas_call(
        update_kernel,
        out_shape=jax.ShapeDtypeStruct((m, n), jnp.float32),
        grid_spec=pltpu.PrefetchScalarGridSpec(
            num_scalar_prefetch=1,
            grid=(m // BLOCK,),
            in_specs=[
                pl.BlockSpec((BLOCK, k), lambda i, s: (i, 0)),
                pl.BlockSpec((n, k), lambda i, s: (0, 0)),
                pl.BlockSpec((n, k), lambda i, s: (0, 0)),
                pl.BlockSpec((BLOCK, n), lambda i, s: (i, 0)),
            ],
            out_specs=pl.BlockSpec((BLOCK, n), lambda i, s: (i, 0)),
            scratch_shapes=[pltpu.VMEM((BLOCK, k), jnp.bfloat16)] * 2,
        ),
        compiler_params=pltpu.CompilerParams(vmem_limit_bytes=60 << 20),
        name="update",
    )(keep, rows, yh, yl, trailing)


def local(front_diag, panel_rows, trailing, pattern):
    diag_factor, panel_factor, yh, yl, rows = factor(front_diag, panel_rows, trailing.shape[1])
    row_blocks, col_blocks = pattern.shape
    row_index = lax.axis_index("row") * row_blocks + jnp.arange(row_blocks)
    col_index = lax.axis_index("col") * col_blocks + jnp.arange(col_blocks)
    keep = pattern * (row_index[:, None] >= col_index[None, :]).astype(jnp.int32)
    schur = update(keep.reshape(-1), rows, yh, yl, trailing)
    return (diag_factor, panel_factor, schur)


def solution(mesh):
    return jax.shard_map(
        local,
        mesh=mesh,
        in_specs=(P(), P(("row", "col"), None), P("row", "col"), P("row", "col")),
        out_specs=(P(), P(("row", "col"), None), P("row", "col")),
        check_vma=False,
    )
```

```python
import jax
import jax.numpy as jnp
from jax import lax
from jax.experimental import pallas as pl
from jax.experimental.pallas import tpu as pltpu
from jax.sharding import PartitionSpec as P

BLOCK = 256
SIDE = 4
GROUP = 512
HI = lax.Precision.HIGHEST
MESH = pl.DeviceIdType.MESH

NT = (((1,), (1,)), ((), ()))
NN = (((1,), (0,)), ((), ()))


def halves(x):
    high = x.astype(jnp.bfloat16)
    return high, (x - high.astype(jnp.float32)).astype(jnp.bfloat16)


def dot3(a, b, dims):
    def one(x, y):
        return lax.dot_general(x, y, dims, preferred_element_type=jnp.float32)
    return one(a[0], b[0]) + (one(a[0], b[1]) + one(a[1], b[0]))


def factor_tile(s, t):
    sub = lax.broadcasted_iota(jnp.int32, (8, 128), 0)
    def wide(x, c):
        return jnp.broadcast_to(x[:, c:c + 1], (8, 128))
    def tall(x, k):
        return jnp.broadcast_to(x[k:k + 1, :], (8, 128))
    n = len(s)
    for g in range(n):
        r, q = s[g], t[g]
        c = [wide(r, 8 * g + m) for m in range(8)]
        u = jnp.zeros((8, 128), jnp.float32)
        w = u
        for k in range(8):
            here = sub == k
            f = c[k]
            p = tall(f, k)
            inv = 1.0 / p
            root = lax.rsqrt(p)
            rk, qk = tall(r, k), tall(q, k)
            u = jnp.where(here, rk * root, u)
            w = jnp.where(here, qk * root, w)
            r = jnp.where(here, rk * inv, r - (f * rk) * inv)
            q = jnp.where(here, qk * inv, q - (f * qk) * inv)
            for m in range(k + 1, 8):
                cm = tall(c[m], k)
                c[m] = jnp.where(here, cm * inv, c[m] - (f * cm) * inv)
        for h in range(g + 1, n):
            sh, th = s[h], t[h]
            ds, dt = None, None
            for m in range(8):
                b = wide(s[h], 8 * g + m)
                a1, a2 = b * tall(r, m), b * tall(q, m)
                ds = a1 if ds is None else ds + a1
                dt = a2 if dt is None else dt + a2
            s[h], t[h] = sh - ds, th - dt
        s[g], t[g] = u, w
    return s, t


def thirds(x):
    f32 = jnp.float32
    h = x.astype(jnp.bfloat16)
    r = x - h.astype(f32)
    m = r.astype(jnp.bfloat16)
    return h, m, (r - m.astype(f32)).astype(jnp.bfloat16)

def wide_left(x):
    h, m, l = thirds(x)
    return jnp.concatenate([h, h, m, m, h, l], axis=1)

def tall_right(x):
    h, m, l = thirds(x)
    return jnp.concatenate([h, m, h, m, l, h], axis=0)

def dot6(a, b):
    return jnp.dot(a, b, preferred_element_type=jnp.float32)


class Exchange:
    def __init__(self, own, rows, cols, sems):
        self.own, self.rows, self.cols = own, rows, cols
        self.row_send, self.row_recv, self.col_send, self.col_recv, self.pair_send, self.here = sems
        row, col = lax.axis_index("row"), lax.axis_index("col")
        self.z, self.k, self.y, self.x = row // 2, row % 2, col // SIDE, col % SIDE
        self.piece = own.shape[0]
        self.half = self.piece // 2
        self.quarter = self.piece // 4

    def device(self, dx=0, dy=0, dz=0, dk=0):
        z, k = lax.rem(self.z + dz + SIDE, SIDE), lax.rem(self.k + dk, 2)
        y, x = lax.rem(self.y + dy + SIDE, SIDE), lax.rem(self.x + dx + SIDE, SIDE)
        return (z * 2 + k, y * SIDE + x)

    def greet(self):
        near = [self.device(dx=1), self.device(dx=-1), self.device(dy=1), self.device(dy=-1),
                self.device(dz=1), self.device(dz=-1), self.device(dk=1)]
        barrier = pltpu.get_barrier_semaphore()
        for device in near:
            pl.semaphore_signal(barrier, inc=1, device_id=device, device_id_type=MESH)
        pl.semaphore_wait(barrier, len(near))

    def origin(self, h, a, b):
        dx, dy = (a, b) if h == 0 else (b, a)
        return lax.rem(self.x + dx, SIDE), lax.rem(self.y + dy, SIDE)

    def row_slot(self, h, a, b, q=None):
        x, y = self.origin(h, a, b)
        start = (y * SIDE + x) * self.piece + h * self.half
        if q is None:
            return self.rows.at[pl.ds(pl.multiple_of(start, self.quarter), self.half)]
        return self.rows.at[pl.ds(pl.multiple_of(start + q * self.quarter, self.quarter), self.quarter)]

    def own_half(self, h):
        return self.own.at[pl.ds(h * self.half, self.half)]

    def row_copy(self, h, a, b, q, along, sign):
        to_a = (a - sign) % SIDE if along == 0 else a
        to_b = (b - sign) % SIDE if along == 1 else b
        index = ((h * SIDE + to_a) * SIDE + to_b) * 2 + (q or 0)
        slot = self.row_slot(h, a, b, q)
        src = self.own_half(h) if (a, b) == (0, 0) else slot
        on_x = (along == 0) == (h == 0)
        device = self.device(dx=sign) if on_x else self.device(dy=sign)
        return pltpu.make_async_remote_copy(
            src_ref=src, dst_ref=slot, send_sem=self.row_send.at[index], recv_sem=self.row_recv.at[index],
            device_id=device, device_id_type=MESH)

    def row_wait(self, h, a, b, q=None):
        index = ((h * SIDE + a) * SIDE + b) * 2 + (q or 0)
        slot = self.row_slot(h, a, b, q)
        pltpu.make_async_copy(slot, slot, self.row_recv.at[index]).wait()

    def sends(self):
        out = []
        for h in (0, 1):
            for sign in (1, -1):
                out.append((0, h, 0, 0, None, 0, sign))
        for h in (0, 1):
            for sign in (1, -1):
                out.append((0, h, 0, 0, None, 1, sign))
        for h in (0, 1):
            out += [(1, h, 3, 0, 0, 0, 1), (1, h, 1, 0, 1, 0, -1)]
        for h in (0, 1):
            for a in (1, 3):
                for sign in (1, -1):
                    out.append((1, h, a, 0, None, 1, sign))
        for h in (0, 1):
            for sign in (1, -1):
                out.append((2, h, 2, 0, None, 1, sign))
        for wave, places in ((2, (0,)), (3, (1, 3)), (4, (2,))):
            for h in (0, 1):
                for a in places:
                    out += [(wave, h, a, 3, 0, 1, 1), (wave, h, a, 1, 1, 1, -1)]
        return out

    ARRIVALS = (
        (),
        ((1, 0), (3, 0)),
        ((2, 0), (0, 1), (0, 3)),
        ((1, 1), (1, 3), (3, 1), (3, 3)),
        ((2, 1), (2, 3), (0, 2)),
        ((1, 2), (3, 2), (2, 2)),
    )

    def col_slot(self, h, a, b):
        x, y = self.origin(h, a, b)
        start = (lax.rem(y, 2) * SIDE + x) * self.piece + h * self.half
        return self.cols.at[pl.ds(pl.multiple_of(start, self.half), self.half)]

    def col_index(self, h, a, b):
        return (h * SIDE + a) * SIDE + b

    def in_cols(self, h, a, b):
        _, y = self.origin(h, a, b)
        return y // 2 == lax.rem(self.x, 2)

    def holder(self):
        return self.k == self.x // 2

    def at_hop(self, h, hop):
        if h == 0:
            return self.z - self.y == hop
        return (lax.rem(self.y - self.z + SIDE, SIDE) == hop) & (self.y < SIDE - 1)

    def goes_on(self, h):
        if h == 0:
            return (self.z >= self.y) & (self.z < SIDE - 1)
        return (lax.rem(self.y - self.z + SIDE, SIDE) < SIDE - 1) & (self.y < SIDE - 1)

    def needed(self):
        return self.z >= self.y

    def col_source(self, h, a, b, first):
        if not first:
            return self.col_slot(h, a, b)
        return self.own_half(h) if (a, b) == (0, 0) else self.row_slot(h, a, b)

    def along(self, h, a, b, first):
        index = self.col_index(h, a, b)
        return pltpu.make_async_remote_copy(
            src_ref=self.col_source(h, a, b, first), dst_ref=self.col_slot(h, a, b),
            send_sem=self.col_send.at[index], recv_sem=self.col_recv.at[index],
            device_id=self.device(dz=1 if h == 0 else -1), device_id_type=MESH)

    def across(self, h, a, b, first):
        index = self.col_index(h, a, b)
        return pltpu.make_async_remote_copy(
            src_ref=self.col_source(h, a, b, first), dst_ref=self.col_slot(h, a, b),
            send_sem=self.pair_send.at[index], recv_sem=self.col_recv.at[index],
            device_id=self.device(dk=1), device_id_type=MESH)

    def keep_copy(self, h, a, b):
        src = self.col_source(h, a, b, True)
        return pltpu.make_async_copy(src, self.col_slot(h, a, b), self.here.at[self.col_index(h, a, b)])

    def col_wait(self, h, a, b):
        slot = self.col_slot(h, a, b)
        pltpu.make_async_copy(slot, slot, self.col_recv.at[self.col_index(h, a, b)]).wait()

    def pieces(self, wave):
        return [(h, a, b) for h in (0, 1) for a, b in (((0, 0),) if wave == 0 else self.ARRIVALS[wave])]

    def start_rows(self, wave):
        for h in (0, 1):
            for a, b in self.ARRIVALS[wave]:
                if b == 2 or (a == 2 and b == 0):
                    self.row_wait(h, a, b, 0)
                    self.row_wait(h, a, b, 1)
                else:
                    self.row_wait(h, a, b)
        for entry in self.sends():
            if entry[0] == wave:
                self.row_copy(*entry[1:]).start()

    def start_cols(self, wave):
        for h, a, b in self.pieces(wave):
            inside = self.in_cols(h, a, b) & self.holder() & (self.z == self.y)

            @pl.when(inside)
            def _():
                self.across(h, a, b, True).start()
                self.keep_copy(h, a, b).start()

            @pl.when(inside & (self.z < SIDE - 1))
            def _():
                self.along(h, a, b, True).start()

    def relay_cols(self, h, a, b, hop):
        here = self.in_cols(h, a, b) & self.holder() & self.at_hop(h, hop)

        @pl.when(here)
        def _():
            self.col_wait(h, a, b)

        @pl.when(here & self.goes_on(h))
        def _():
            self.along(h, a, b, False).start()

        @pl.when(here & self.needed())
        def _():
            self.across(h, a, b, False).start()

    def finish_cols(self):
        for wave in range(len(self.ARRIVALS)):
            for h, a, b in self.pieces(wave):
                inside = self.in_cols(h, a, b) & self.needed()

                @pl.when(inside & self.holder() & (self.z == self.y))
                def _():
                    self.keep_copy(h, a, b).wait()

                @pl.when(inside & jnp.logical_not(self.holder()))
                def _():
                    self.col_wait(h, a, b)

    def finish(self):
        for entry in self.sends():
            self.row_copy(*entry[1:]).wait_send()
        for wave in range(len(self.ARRIVALS)):
            for h, a, b in self.pieces(wave):
                inside = self.in_cols(h, a, b) & self.holder()

                @pl.when(inside & self.needed())
                def _():
                    self.across(h, a, b, False).wait_send()

                @pl.when(inside & self.goes_on(h))
                def _():
                    self.along(h, a, b, False).wait_send()


ROW_POINTS = (0, 1, 3, 5, 6, 8)
POINTS = [0.0] + [2.5 + 5.6 * (k + 1) for k in range(8)] + [48.5 + 0.65 * i for i in range(33)]


def relay_points():
    table = {}
    for kind in ((0, 1), (2, 3), (3, 0), (1, 2)):
        for h in (0, 1):
            free = [0.0] * (SIDE - 1)
            for wave, places in enumerate(Exchange.ARRIVALS):
                for a, b in (((0, 0),) if wave == 0 else places):
                    if (b if h == 0 else a) not in kind:
                        continue
                    ready = POINTS[ROW_POINTS[wave]]
                    for hop in range(1, SIDE):
                        free[hop - 1] = max(ready, free[hop - 1]) + 2.8
                        arrival = free[hop - 1] + 1.8
                        point = min([i for i, t in enumerate(POINTS) if t >= arrival], default=len(POINTS) - 1)
                        ready = POINTS[point]
                        table[h, a, b, hop] = max(point, table.get((h, a, b, hop), 0))
    return table


RELAYS = relay_points()


def transfers(exchange, point):
    for wave, at in enumerate(ROW_POINTS):
        if at == point:
            exchange.start_rows(wave)
            exchange.start_cols(wave)
    for (h, a, b, hop), at in RELAYS.items():
        if at == point:
            exchange.relay_cols(h, a, b, hop)


def factor_kernel(a_ref, own_ref, l_ref, x_ref, yh_ref, yl_ref, ch_ref, cl_ref, rows_ref,
                  w_ref, g_ref, d_ref, u_ref, wd_ref, cols_ref, wh, wl, r_buf, zf, zh, zl, yh_buf, yl_buf,
                  sem_a, sem_own, sem_in, sem_out, *sems):
    n = a_ref.shape[0]
    nb = n // 128
    load = pltpu.make_async_copy(a_ref, w_ref, sem_a)
    load.start()
    exchange = Exchange(own_ref, rows_ref, cols_ref, sems)
    l_ref[...] = jnp.zeros_like(l_ref)
    wd_ref[...] = jnp.zeros_like(wd_ref)
    u_ref[...] = jnp.zeros_like(u_ref)
    exchange.greet()
    me = lax.axis_index("col")
    first = pl.multiple_of(me * own_ref.shape[0], own_ref.shape[0])
    keep_own = pltpu.make_async_copy(own_ref, rows_ref.at[pl.ds(first, own_ref.shape[0])], sem_own)
    transfers(exchange, 0)
    keep_own.start()
    load.wait()
    d_ref[...] = w_ref[:128, :128]
    sub = lax.broadcasted_iota(jnp.int32, (8, 128), 0)
    lane = lax.broadcasted_iota(jnp.int32, (8, 128), 1)
    lane_all = lax.broadcasted_iota(jnp.int32, (128, n), 1)

    def settle(p, last):
        q = jnp.maximum(p - 1, 0)
        oq = pl.multiple_of(q * 128, 128)
        wd = wd_ref[...]
        row = w_ref[pl.ds(oq, 128), :]
        g = dot6(wide_left(wd), tall_right(row))
        inside = (lane_all >= oq) & (lane_all < oq + 128)
        done = jnp.where(lane_all < oq, g, 0.0)
        w_ref[pl.ds(oq, 128), :] = done if last else jnp.where(p > 0, done, row)
        l_ref[pl.ds(oq, 128), pl.ds(oq, 128)] = u_ref[...].T
        if last:
            w_ref[pl.ds(oq, 128), pl.ds(oq, 128)] = wd
            return
        g_ref[...] = g
        g_ref[:, pl.ds(oq, 128)] += wd
        right = tall_right(g_ref[...])
        for i in range(1, nb):
            li = jnp.where(q < i, g[:, i * 128:(i + 1) * 128], 0.0).T
            l_ref[i * 128:(i + 1) * 128, pl.ds(oq, 128)] = jnp.where(q < i, li, l_ref[i * 128:(i + 1) * 128, pl.ds(oq, 128)])
            w_ref[i * 128:(i + 1) * 128, :] -= dot6(wide_left(li), right)
        w_ref[pl.ds(oq, 128), pl.ds(oq, 128)] = jnp.where(p > 0, wd, w_ref[pl.ds(oq, 128), pl.ds(oq, 128)])

    def panel(p, carry):
        o = pl.multiple_of(p * 128, 128)
        o1 = pl.multiple_of(jnp.minimum(p + 1, nb - 1) * 128, 128)
        s = [d_ref[8 * g:8 * g + 8, :] for g in range(16)]
        t = [(lane == sub + 8 * g).astype(jnp.float32) for g in range(16)]
        s, t = factor_tile(s, t)
        settle(p, False)
        for g in range(16):
            u_ref[8 * g:8 * g + 8, :] = jnp.where(lane >= sub + 8 * g, s[g], 0.0)
            wd_ref[8 * g:8 * g + 8, :] = t[g]
        un = dot6(wide_left(wd_ref[...]), tall_right(w_ref[pl.ds(o, 128), pl.ds(o1, 128)]))
        d_ref[...] = w_ref[pl.ds(o1, 128), pl.ds(o1, 128)] - dot6(wide_left(un.T), tall_right(un))
        for k in range(nb):
            @pl.when(p == k)
            def _():
                transfers(exchange, k + 1)
        return carry
    lax.fori_loop(0, nb, panel, 0)
    keep_own.wait()

    def fetch(b, slot):
        rows = rows_ref.at[pl.ds(pl.multiple_of(b * GROUP, GROUP), GROUP)]
        return pltpu.make_async_copy(rows, r_buf.at[slot], sem_in.at[slot])

    def store(b, slot):
        part = pl.ds(pl.multiple_of(b * GROUP, GROUP), GROUP)
        return (pltpu.make_async_copy(yh_buf.at[slot], yh_ref.at[part], sem_out.at[slot, 0]),
                pltpu.make_async_copy(yl_buf.at[slot], yl_ref.at[part], sem_out.at[slot, 1]))

    blocks = rows_ref.shape[0] // GROUP
    fetch(0, 0).start()
    settle(nb, True)
    wh[...], wl[...] = halves(w_ref[...])

    def passing(b, j):
        for k in range(blocks):
            if any(at == nb + 1 + 8 * k + j for at in RELAYS.values()):
                @pl.when(b == k)
                def _():
                    transfers(exchange, nb + 1 + 8 * k + j)

    def transform(b, carry):
        slot = lax.rem(b, 2)
        fetch(b, slot).wait()

        @pl.when(b + 1 < blocks)
        def _():
            fetch(b + 1, 1 - slot).start()

        @pl.when(b >= 2)
        def _():
            for copy in store(b - 2, slot):
                copy.wait()
        rh, rl = halves(r_buf[slot])
        zh[...], zl[...] = rh, rl
        for j, p in enumerate(range(0, n, BLOCK)):
            e = p + BLOCK
            zf[:, p:e] = dot3((zh[:, :e], zl[:, :e]), (wh[p:e, :e], wl[p:e, :e]), NT)
            passing(b, j)
        per = GROUP // own_ref.shape[0]

        @pl.when(me // per == b)
        def _():
            x_ref[...] = zf[pl.ds(pl.multiple_of(lax.rem(me, per) * own_ref.shape[0], own_ref.shape[0]), own_ref.shape[0]), :]
        rh, rl = halves(zf[...])
        zh[...], zl[...] = rh, rl
        for j, p in enumerate(range(0, n, BLOCK)):
            e = p + BLOCK
            y = dot3((zh[:, p:], zl[:, p:]), (wh[p:, p:e], wl[p:, p:e]), NN)
            yh_buf[slot, :, p:e], yl_buf[slot, :, p:e] = halves(y)
            passing(b, 4 + j)
        for copy in store(b, slot):
            copy.start()
        return carry
    lax.fori_loop(0, blocks, transform, 0)
    transfers(exchange, len(POINTS) - 1)
    exchange.finish_cols()
    ch_ref[...], cl_ref[...] = halves(cols_ref[...])
    exchange.finish()
    for b in (blocks - 2, blocks - 1):
        for copy in store(b, b % 2):
            copy.wait()


def factor(front_diag, own, cols):
    f32, bf = jnp.float32, jnp.bfloat16
    n = front_diag.shape[0]
    rows = lax.axis_size("col") * own.shape[0]
    vm, anywhere = pl.BlockSpec(memory_space=pltpu.VMEM), pl.BlockSpec(memory_space=pl.ANY)
    dma = pltpu.SemaphoreType.DMA
    return pl.pallas_call(
        factor_kernel,
        out_shape=(
            jax.ShapeDtypeStruct((n, n), f32),
            jax.ShapeDtypeStruct(own.shape, f32),
            jax.ShapeDtypeStruct((rows, n), bf),
            jax.ShapeDtypeStruct((rows, n), bf),
            jax.ShapeDtypeStruct((cols, n), bf),
            jax.ShapeDtypeStruct((cols, n), bf),
            jax.ShapeDtypeStruct((rows, n), f32),
        ),
        in_specs=[anywhere, vm],
        out_specs=(vm, vm, anywhere, anywhere, vm, vm, anywhere),
        scratch_shapes=[
            pltpu.VMEM((n, n), f32), pltpu.VMEM((128, n), f32),
            pltpu.VMEM((128, 128), f32), pltpu.VMEM((128, 128), f32), pltpu.VMEM((128, 128), f32),
            pltpu.VMEM((cols, n), f32),
            pltpu.VMEM((n, n), bf), pltpu.VMEM((n, n), bf),
            pltpu.VMEM((2, GROUP, n), f32), pltpu.VMEM((GROUP, n), f32),
            pltpu.VMEM((GROUP, n), bf), pltpu.VMEM((GROUP, n), bf),
            pltpu.VMEM((2, GROUP, n), bf), pltpu.VMEM((2, GROUP, n), bf),
            dma, dma, dma((2,)), dma((2, 2)),
            dma((64,)), dma((64,)), dma((32,)), dma((32,)), dma((32,)), dma((32,)),
        ],
        compiler_params=pltpu.CompilerParams(vmem_limit_bytes=56 << 20, collective_id=0, has_side_effects=True),
        name="factor",
    )(front_diag, own)


def update_kernel(keep_ref, rh_ref, rl_ref, ch_ref, cl_ref, t_ref, l_ref, x_ref, o_ref, lo_ref, xo_ref):
    i = pl.program_id(0)
    lo_ref[...] = l_ref[...]
    xo_ref[...] = x_ref[...]
    cols = o_ref.shape[1] // BLOCK
    for j in range(cols):
        part = slice(j * BLOCK, (j + 1) * BLOCK)
        kept = keep_ref[i * cols + j] != 0

        @pl.when(kept)
        def _():
            d = dot3((rh_ref[...], rl_ref[...]), (ch_ref[part, :], cl_ref[part, :]), NT)
            o_ref[:, part] = t_ref[:, part] - d

        @pl.when(jnp.logical_not(kept))
        def _():
            o_ref[:, part] = t_ref[:, part]


def update(keep, rh, rl, ch, cl, trailing, diag_factor, panel_factor):
    m, n = trailing.shape
    k = rh.shape[1]
    steps = m // BLOCK
    row = lambda size, width: pl.BlockSpec((size, width), lambda i, s: (i, 0))
    whole = lambda size, width: pl.BlockSpec((size, width), lambda i, s: (0, 0))
    ld, lx = diag_factor.shape[0] // steps, panel_factor.shape[0] // steps
    return pl.pallas_call(
        update_kernel,
        out_shape=(jax.ShapeDtypeStruct((m, n), jnp.float32), jax.ShapeDtypeStruct(diag_factor.shape, jnp.float32),
                   jax.ShapeDtypeStruct(panel_factor.shape, jnp.float32)),
        grid_spec=pltpu.PrefetchScalarGridSpec(
            num_scalar_prefetch=1,
            grid=(steps,),
            in_specs=[row(BLOCK, k), row(BLOCK, k), whole(n, k), whole(n, k), row(BLOCK, n), row(ld, k), row(lx, k)],
            out_specs=(row(BLOCK, n), row(ld, k), row(lx, k)),
        ),
        compiler_params=pltpu.CompilerParams(vmem_limit_bytes=60 << 20),
        name="update",
    )(keep, rh, rl, ch, cl, trailing, diag_factor, panel_factor)


def local(front_diag, panel_rows, trailing, pattern):
    row_blocks, col_blocks = pattern.shape
    row_index = lax.axis_index("row") * row_blocks + jnp.arange(row_blocks)
    col_index = lax.axis_index("col") * col_blocks + jnp.arange(col_blocks)
    keep = pattern * (row_index[:, None] >= col_index[None, :]).astype(jnp.int32)
    diag_factor, panel_factor, yh, yl, ch, cl, _ = factor(front_diag, panel_rows, trailing.shape[1])
    schur, diag_factor, panel_factor = update(keep.reshape(-1), yh, yl, ch, cl, trailing, diag_factor, panel_factor)
    return (diag_factor, panel_factor, schur)


def solution(mesh):
    return jax.shard_map(
        local,
        mesh=mesh,
        in_specs=(P(), P(("row", "col"), None), P("row", "col"), P("row", "col")),
        out_specs=(P(), P(("row", "col"), None), P("row", "col")),
        check_vma=False,
    )
```

```python
import jax
import jax.numpy as jnp
from jax import lax
from jax.experimental import pallas as pl
from jax.experimental.pallas import tpu as pltpu
from jax.sharding import PartitionSpec as P

BLOCK = 256
SIDE = 4
GROUP = 512
HI = lax.Precision.HIGHEST
MESH = pl.DeviceIdType.MESH

NT = (((1,), (1,)), ((), ()))
NN = (((1,), (0,)), ((), ()))


def halves(x):
    high = x.astype(jnp.bfloat16)
    return high, (x - high.astype(jnp.float32)).astype(jnp.bfloat16)


def dot3(a, b, dims):
    def one(x, y):
        return lax.dot_general(x, y, dims, preferred_element_type=jnp.float32)
    return one(a[0], b[0]) + (one(a[0], b[1]) + one(a[1], b[0]))


def factor_tile(s, t):
    sub = lax.broadcasted_iota(jnp.int32, (8, 128), 0)
    def wide(x, c):
        return jnp.broadcast_to(x[:, c:c + 1], (8, 128))
    def tall(x, k):
        return jnp.broadcast_to(x[k:k + 1, :], (8, 128))
    n = len(s)
    for g in range(n):
        r, q = s[g], t[g]
        c = [wide(r, 8 * g + m) for m in range(8)]
        u = jnp.zeros((8, 128), jnp.float32)
        w = u
        for k in range(8):
            here = sub == k
            f = c[k]
            p = tall(f, k)
            inv = 1.0 / p
            root = lax.rsqrt(p)
            rk, qk = tall(r, k), tall(q, k)
            u = jnp.where(here, rk * root, u)
            w = jnp.where(here, qk * root, w)
            r = jnp.where(here, rk * inv, r - (f * rk) * inv)
            q = jnp.where(here, qk * inv, q - (f * qk) * inv)
            for m in range(k + 1, 8):
                cm = tall(c[m], k)
                c[m] = jnp.where(here, cm * inv, c[m] - (f * cm) * inv)
        for h in range(g + 1, n):
            sh, th = s[h], t[h]
            ds, dt = None, None
            for m in range(8):
                b = wide(s[h], 8 * g + m)
                a1, a2 = b * tall(r, m), b * tall(q, m)
                ds = a1 if ds is None else ds + a1
                dt = a2 if dt is None else dt + a2
            s[h], t[h] = sh - ds, th - dt
        s[g], t[g] = u, w
    return s, t


def thirds(x):
    f32 = jnp.float32
    h = x.astype(jnp.bfloat16)
    r = x - h.astype(f32)
    m = r.astype(jnp.bfloat16)
    return h, m, (r - m.astype(f32)).astype(jnp.bfloat16)

def wide_left(x):
    h, m, l = thirds(x)
    return jnp.concatenate([h, h, m, m, h, l], axis=1)

def tall_right(x):
    h, m, l = thirds(x)
    return jnp.concatenate([h, m, h, m, l, h], axis=0)

def dot6(a, b):
    return jnp.dot(a, b, preferred_element_type=jnp.float32)


class Exchange:
    def __init__(self, own, rows, cols, sems):
        self.own, self.rows, self.cols = own, rows, cols
        self.row_send, self.row_recv, self.col_send, self.col_recv, self.pair_send, self.here = sems
        row, col = lax.axis_index("row"), lax.axis_index("col")
        self.z, self.k, self.y, self.x = row // 2, row % 2, col // SIDE, col % SIDE
        self.piece = own.shape[0]
        self.half = self.piece // 2
        self.quarter = self.piece // 4

    def device(self, dx=0, dy=0, dz=0, dk=0):
        z, k = lax.rem(self.z + dz + SIDE, SIDE), lax.rem(self.k + dk, 2)
        y, x = lax.rem(self.y + dy + SIDE, SIDE), lax.rem(self.x + dx + SIDE, SIDE)
        return (z * 2 + k, y * SIDE + x)

    def greet(self):
        near = [self.device(dx=1), self.device(dx=-1), self.device(dy=1), self.device(dy=-1),
                self.device(dz=1), self.device(dz=-1), self.device(dk=1)]
        barrier = pltpu.get_barrier_semaphore()
        for device in near:
            pl.semaphore_signal(barrier, inc=1, device_id=device, device_id_type=MESH)
        pl.semaphore_wait(barrier, len(near))

    def origin(self, h, a, b):
        dx, dy = (a, b) if h == 0 else (b, a)
        return lax.rem(self.x + dx, SIDE), lax.rem(self.y + dy, SIDE)

    def row_slot(self, h, a, b, q=None):
        x, y = self.origin(h, a, b)
        start = (y * SIDE + x) * self.piece + h * self.half
        if q is None:
            return self.rows.at[pl.ds(pl.multiple_of(start, self.quarter), self.half)]
        return self.rows.at[pl.ds(pl.multiple_of(start + q * self.quarter, self.quarter), self.quarter)]

    def own_half(self, h):
        return self.own.at[pl.ds(h * self.half, self.half)]

    def row_copy(self, h, a, b, q, along, sign):
        to_a = (a - sign) % SIDE if along == 0 else a
        to_b = (b - sign) % SIDE if along == 1 else b
        index = ((h * SIDE + to_a) * SIDE + to_b) * 2 + (q or 0)
        slot = self.row_slot(h, a, b, q)
        src = self.own_half(h) if (a, b) == (0, 0) else slot
        on_x = (along == 0) == (h == 0)
        device = self.device(dx=sign) if on_x else self.device(dy=sign)
        return pltpu.make_async_remote_copy(
            src_ref=src, dst_ref=slot, send_sem=self.row_send.at[index], recv_sem=self.row_recv.at[index],
            device_id=device, device_id_type=MESH)

    def row_wait(self, h, a, b, q=None):
        index = ((h * SIDE + a) * SIDE + b) * 2 + (q or 0)
        slot = self.row_slot(h, a, b, q)
        pltpu.make_async_copy(slot, slot, self.row_recv.at[index]).wait()

    def sends(self):
        out = []
        for h in (0, 1):
            for sign in (1, -1):
                out.append((0, h, 0, 0, None, 0, sign))
        for h in (0, 1):
            for sign in (1, -1):
                out.append((0, h, 0, 0, None, 1, sign))
        for h in (0, 1):
            out += [(1, h, 3, 0, 0, 0, 1), (1, h, 1, 0, 1, 0, -1)]
        for h in (0, 1):
            for a in (1, 3):
                for sign in (1, -1):
                    out.append((1, h, a, 0, None, 1, sign))
        for h in (0, 1):
            for sign in (1, -1):
                out.append((2, h, 2, 0, None, 1, sign))
        for wave, places in ((2, (0,)), (3, (1, 3)), (4, (2,))):
            for h in (0, 1):
                for a in places:
                    out += [(wave, h, a, 3, 0, 1, 1), (wave, h, a, 1, 1, 1, -1)]
        return out

    ARRIVALS = (
        (),
        ((1, 0), (3, 0)),
        ((2, 0), (0, 1), (0, 3)),
        ((1, 1), (1, 3), (3, 1), (3, 3)),
        ((2, 1), (2, 3), (0, 2)),
        ((1, 2), (3, 2), (2, 2)),
    )

    def col_slot(self, h, a, b):
        x, y = self.origin(h, a, b)
        start = (lax.rem(y, 2) * SIDE + x) * self.piece + h * self.half
        return self.cols.at[pl.ds(pl.multiple_of(start, self.half), self.half)]

    def col_index(self, h, a, b):
        return (h * SIDE + a) * SIDE + b

    def in_cols(self, h, a, b):
        _, y = self.origin(h, a, b)
        return y // 2 == lax.rem(self.x, 2)

    def holder(self):
        return self.k == self.x // 2

    def at_hop(self, h, hop):
        if h == 0:
            return self.z - self.y == hop
        return (lax.rem(self.y - self.z + SIDE, SIDE) == hop) & (self.y < SIDE - 1)

    def goes_on(self, h):
        if h == 0:
            return (self.z >= self.y) & (self.z < SIDE - 1)
        return (lax.rem(self.y - self.z + SIDE, SIDE) < SIDE - 1) & (self.y < SIDE - 1)

    def needed(self):
        return self.z >= self.y

    def col_source(self, h, a, b, first):
        if not first:
            return self.col_slot(h, a, b)
        return self.own_half(h) if (a, b) == (0, 0) else self.row_slot(h, a, b)

    def along(self, h, a, b, first):
        index = self.col_index(h, a, b)
        return pltpu.make_async_remote_copy(
            src_ref=self.col_source(h, a, b, first), dst_ref=self.col_slot(h, a, b),
            send_sem=self.col_send.at[index], recv_sem=self.col_recv.at[index],
            device_id=self.device(dz=1 if h == 0 else -1), device_id_type=MESH)

    def across(self, h, a, b, first):
        index = self.col_index(h, a, b)
        return pltpu.make_async_remote_copy(
            src_ref=self.col_source(h, a, b, first), dst_ref=self.col_slot(h, a, b),
            send_sem=self.pair_send.at[index], recv_sem=self.col_recv.at[index],
            device_id=self.device(dk=1), device_id_type=MESH)

    def keep_copy(self, h, a, b):
        src = self.col_source(h, a, b, True)
        return pltpu.make_async_copy(src, self.col_slot(h, a, b), self.here.at[self.col_index(h, a, b)])

    def col_wait(self, h, a, b):
        slot = self.col_slot(h, a, b)
        pltpu.make_async_copy(slot, slot, self.col_recv.at[self.col_index(h, a, b)]).wait()

    def pieces(self, wave):
        return [(h, a, b) for h in (0, 1) for a, b in (((0, 0),) if wave == 0 else self.ARRIVALS[wave])]

    def start_rows(self, wave):
        for h in (0, 1):
            for a, b in self.ARRIVALS[wave]:
                if b == 2 or (a == 2 and b == 0):
                    self.row_wait(h, a, b, 0)
                    self.row_wait(h, a, b, 1)
                else:
                    self.row_wait(h, a, b)
        for entry in self.sends():
            if entry[0] == wave:
                self.row_copy(*entry[1:]).start()

    def start_cols(self, wave):
        for h, a, b in self.pieces(wave):
            inside = self.in_cols(h, a, b) & self.holder() & (self.z == self.y)

            @pl.when(inside)
            def _():
                self.across(h, a, b, True).start()
                self.keep_copy(h, a, b).start()

            @pl.when(inside & (self.z < SIDE - 1))
            def _():
                self.along(h, a, b, True).start()

    def relay_cols(self, h, a, b, hop):
        here = self.in_cols(h, a, b) & self.holder() & self.at_hop(h, hop)

        @pl.when(here)
        def _():
            self.col_wait(h, a, b)

        @pl.when(here & self.goes_on(h))
        def _():
            self.along(h, a, b, False).start()

        @pl.when(here & self.needed())
        def _():
            self.across(h, a, b, False).start()

    def finish_cols(self):
        for wave in range(len(self.ARRIVALS)):
            for h, a, b in self.pieces(wave):
                inside = self.in_cols(h, a, b) & self.needed()

                @pl.when(inside & self.holder() & (self.z == self.y))
                def _():
                    self.keep_copy(h, a, b).wait()

                @pl.when(inside & jnp.logical_not(self.holder()))
                def _():
                    self.col_wait(h, a, b)

    def finish(self):
        for entry in self.sends():
            self.row_copy(*entry[1:]).wait_send()
        for wave in range(len(self.ARRIVALS)):
            for h, a, b in self.pieces(wave):
                inside = self.in_cols(h, a, b) & self.holder()

                @pl.when(inside & self.needed())
                def _():
                    self.across(h, a, b, False).wait_send()

                @pl.when(inside & self.goes_on(h))
                def _():
                    self.along(h, a, b, False).wait_send()


ROW_POINTS = (0, 1, 3, 5, 6, 8)
STEPS = 4
POINTS = [0.0] + [2.5 + 5.6 * (k + 1) for k in range(8)] + [49.5 + 0.65 * i for i in range(16)] + [60.5 + 0.7 * i for i in range(40)]


def relay_points():
    table = {}
    for kind in ((0, 1), (2, 3), (3, 0), (1, 2)):
        for h in (0, 1):
            free = [0.0] * (SIDE - 1)
            for wave, places in enumerate(Exchange.ARRIVALS):
                for a, b in (((0, 0),) if wave == 0 else places):
                    if (b if h == 0 else a) not in kind:
                        continue
                    ready = POINTS[ROW_POINTS[wave]]
                    for hop in range(1, SIDE):
                        free[hop - 1] = max(ready, free[hop - 1]) + 2.8
                        arrival = free[hop - 1] + 1.8
                        point = min([i for i, t in enumerate(POINTS) if t >= arrival], default=len(POINTS) - 1)
                        ready = POINTS[point]
                        table[h, a, b, hop] = max(point, table.get((h, a, b, hop), 0))
    return table


RELAYS = relay_points()


def transfers(exchange, point):
    for wave, at in enumerate(ROW_POINTS):
        if at == point:
            exchange.start_rows(wave)
            exchange.start_cols(wave)
    for (h, a, b, hop), at in RELAYS.items():
        if at == point:
            exchange.relay_cols(h, a, b, hop)


def factor_kernel(a_ref, own_in, l_out, x_ref, yh_ref, yl_ref, zh_ref, zl_ref, rows_ref,
                  w_ref, l_ref, g_ref, d_ref, u_ref, wd_ref, cols_ref, wh, wl, r_buf, zf, rh, rl, yh_buf, yl_buf,
                  ch, cl, zh_buf, zl_buf, own_ref, sem_a, sem_own, sem_l, sem_in, sem_out, sem_z, *sems):
    n = a_ref.shape[0]
    nb = n // 128
    load_own = pltpu.make_async_copy(own_in, own_ref, sem_own)
    load_own.start()
    load = pltpu.make_async_copy(a_ref, w_ref, sem_a)
    load.start()
    exchange = Exchange(own_ref, rows_ref, cols_ref, sems)
    l_ref[...] = jnp.zeros_like(l_ref)
    wd_ref[...] = jnp.zeros_like(wd_ref)
    u_ref[...] = jnp.zeros_like(u_ref)
    exchange.greet()
    load_own.wait()
    me = lax.axis_index("col")
    first = pl.multiple_of(me * own_ref.shape[0], own_ref.shape[0])
    keep_own = pltpu.make_async_copy(own_ref, rows_ref.at[pl.ds(first, own_ref.shape[0])], sem_own)
    transfers(exchange, 0)
    keep_own.start()
    load.wait()
    d_ref[...] = w_ref[:128, :128]
    sub = lax.broadcasted_iota(jnp.int32, (8, 128), 0)
    lane = lax.broadcasted_iota(jnp.int32, (8, 128), 1)
    lane_all = lax.broadcasted_iota(jnp.int32, (128, n), 1)

    def settle(p, last):
        q = jnp.maximum(p - 1, 0)
        oq = pl.multiple_of(q * 128, 128)
        wd = wd_ref[...]
        row = w_ref[pl.ds(oq, 128), :]
        g = dot6(wide_left(wd), tall_right(row))
        inside = (lane_all >= oq) & (lane_all < oq + 128)
        done = jnp.where(lane_all < oq, g, 0.0)
        w_ref[pl.ds(oq, 128), :] = done if last else jnp.where(p > 0, done, row)
        l_ref[pl.ds(oq, 128), pl.ds(oq, 128)] = u_ref[...].T
        if last:
            w_ref[pl.ds(oq, 128), pl.ds(oq, 128)] = wd
            return
        g_ref[...] = g
        g_ref[:, pl.ds(oq, 128)] += wd
        right = tall_right(g_ref[...])
        for i in range(1, nb):
            li = jnp.where(q < i, g[:, i * 128:(i + 1) * 128], 0.0).T
            l_ref[i * 128:(i + 1) * 128, pl.ds(oq, 128)] = jnp.where(q < i, li, l_ref[i * 128:(i + 1) * 128, pl.ds(oq, 128)])
            w_ref[i * 128:(i + 1) * 128, :] -= dot6(wide_left(li), right)
        w_ref[pl.ds(oq, 128), pl.ds(oq, 128)] = jnp.where(p > 0, wd, w_ref[pl.ds(oq, 128), pl.ds(oq, 128)])

    def panel(p, carry):
        o = pl.multiple_of(p * 128, 128)
        o1 = pl.multiple_of(jnp.minimum(p + 1, nb - 1) * 128, 128)
        s = [d_ref[8 * g:8 * g + 8, :] for g in range(16)]
        t = [(lane == sub + 8 * g).astype(jnp.float32) for g in range(16)]
        s, t = factor_tile(s, t)
        settle(p, False)
        for g in range(16):
            u_ref[8 * g:8 * g + 8, :] = jnp.where(lane >= sub + 8 * g, s[g], 0.0)
            wd_ref[8 * g:8 * g + 8, :] = t[g]
        un = dot6(wide_left(wd_ref[...]), tall_right(w_ref[pl.ds(o, 128), pl.ds(o1, 128)]))
        d_ref[...] = w_ref[pl.ds(o1, 128), pl.ds(o1, 128)] - dot6(wide_left(un.T), tall_right(un))
        for k in range(nb):
            @pl.when(p == k)
            def _():
                transfers(exchange, k + 1)
        return carry
    lax.fori_loop(0, nb, panel, 0)
    keep_own.wait()

    def fetch(b, slot):
        rows = rows_ref.at[pl.ds(pl.multiple_of(b * GROUP, GROUP), GROUP)]
        return pltpu.make_async_copy(rows, r_buf.at[slot], sem_in.at[slot])

    def store(b, slot):
        part = pl.ds(pl.multiple_of(b * GROUP, GROUP), GROUP)
        return (pltpu.make_async_copy(yh_buf.at[slot], yh_ref.at[part], sem_out.at[slot, 0]),
                pltpu.make_async_copy(yl_buf.at[slot], yl_ref.at[part], sem_out.at[slot, 1]))

    blocks = rows_ref.shape[0] // GROUP
    fetch(0, 0).start()
    settle(nb, True)
    save_l = pltpu.make_async_copy(l_ref, l_out, sem_l)
    save_l.start()
    wh[...], wl[...] = halves(w_ref[...])

    def passing(b, j):
        for k in range(blocks):
            at = nb + 1 + STEPS * k + j
            if at in RELAYS.values():
                @pl.when(b == k)
                def _():
                    transfers(exchange, at)

    def transform(b, carry):
        slot = lax.rem(b, 2)
        fetch(b, slot).wait()

        @pl.when(b + 1 < blocks)
        def _():
            fetch(b + 1, 1 - slot).start()

        @pl.when(b >= 2)
        def _():
            for copy in store(b - 2, slot):
                copy.wait()
        rh[...], rl[...] = halves(r_buf[slot])
        for j, p in enumerate(range(0, n, BLOCK)):
            e = p + BLOCK
            z = dot3((rh[:, :e], rl[:, :e]), (wh[p:e, :e], wl[p:e, :e]), NT)
            zf[:, p:e] = z
            yh_buf[slot, :, p:e], yl_buf[slot, :, p:e] = halves(z)
            passing(b, j)
        for copy in store(b, slot):
            copy.start()
        per = GROUP // own_ref.shape[0]

        @pl.when(me // per == b)
        def _():
            x_ref[...] = zf[pl.ds(pl.multiple_of(lax.rem(me, per) * own_ref.shape[0], own_ref.shape[0]), own_ref.shape[0]), :]
        return carry
    lax.fori_loop(0, blocks, transform, 0)
    for point in range(nb + 1 + STEPS * blocks, len(POINTS)):
        transfers(exchange, point)
    exchange.finish_cols()
    ch[...], cl[...] = halves(cols_ref[...])
    saves = []
    for j, p in enumerate(range(0, n, BLOCK)):
        e = p + BLOCK
        z = dot3((ch[:, :e], cl[:, :e]), (wh[p:e, :e], wl[p:e, :e]), NT)
        zh_buf[:, p:e], zl_buf[:, p:e] = halves(z)
        saves += [pltpu.make_async_copy(zh_buf.at[:, p:e], zh_ref.at[:, p:e], sem_z.at[j, 0]),
                  pltpu.make_async_copy(zl_buf.at[:, p:e], zl_ref.at[:, p:e], sem_z.at[j, 1])]
        saves[-2].start()
        saves[-1].start()
    exchange.finish()
    for b in (blocks - 2, blocks - 1):
        for copy in store(b, b % 2):
            copy.wait()
    for copy in [save_l] + saves:
        copy.wait()


def factor(front_diag, own, cols):
    f32, bf = jnp.float32, jnp.bfloat16
    n = front_diag.shape[0]
    rows = lax.axis_size("col") * own.shape[0]
    vm, anywhere = pl.BlockSpec(memory_space=pltpu.VMEM), pl.BlockSpec(memory_space=pl.ANY)
    hbm = pl.BlockSpec(memory_space=pl.ANY)
    dma = pltpu.SemaphoreType.DMA
    return pl.pallas_call(
        factor_kernel,
        out_shape=(
            jax.ShapeDtypeStruct((n, n), f32),
            jax.ShapeDtypeStruct(own.shape, f32),
            jax.ShapeDtypeStruct((rows, n), bf),
            jax.ShapeDtypeStruct((rows, n), bf),
            jax.ShapeDtypeStruct((cols, n), bf),
            jax.ShapeDtypeStruct((cols, n), bf),
            jax.ShapeDtypeStruct((rows, n), f32),
        ),
        in_specs=[hbm, hbm],
        out_specs=(anywhere, vm, hbm, hbm, anywhere, anywhere, hbm),
        scratch_shapes=[
            pltpu.VMEM((n, n), f32), pltpu.VMEM((n, n), f32), pltpu.VMEM((128, n), f32),
            pltpu.VMEM((128, 128), f32), pltpu.VMEM((128, 128), f32), pltpu.VMEM((128, 128), f32),
            pltpu.VMEM((cols, n), f32),
            pltpu.VMEM((n, n), bf), pltpu.VMEM((n, n), bf),
            pltpu.VMEM((2, GROUP, n), f32), pltpu.VMEM((GROUP, n), f32),
            pltpu.VMEM((GROUP, n), bf), pltpu.VMEM((GROUP, n), bf),
            pltpu.VMEM((2, GROUP, n), bf), pltpu.VMEM((2, GROUP, n), bf),
            pltpu.VMEM((cols, n), bf), pltpu.VMEM((cols, n), bf),
            pltpu.VMEM((cols, n), bf), pltpu.VMEM((cols, n), bf),
            pltpu.VMEM(own.shape, f32),
            dma, dma, dma, dma((2,)), dma((2, 2)), dma((n // BLOCK, 2)),
            dma((64,)), dma((64,)), dma((32,)), dma((32,)), dma((32,)), dma((32,)),
        ],
        compiler_params=pltpu.CompilerParams(vmem_limit_bytes=56 << 20, collective_id=0, has_side_effects=True),
        name="factor",
    )(front_diag, own)


UNIT = 2
AHEAD = 2


def update_kernel(keep_ref, yh_ref, yl_ref, zh_ref, zl_ref, t_ref, l_ref, x_ref, o_ref, lo_ref, xo_ref,
                  yh, yl, zh, zl, t, l, x, sem_z, sem_in, sem_out, sem_l):
    n = t.shape[1]
    size = UNIT * BLOCK
    steps, cols = t.shape[0] // size, n // BLOCK

    def inputs(i):
        part = slice(i * size, (i + 1) * size)
        return [pltpu.make_async_copy(a.at[part], b.at[part], sem_in.at[i, k])
                for k, (a, b) in enumerate(((yh_ref, yh), (yl_ref, yl), (t_ref, t)))]
    factors = [pltpu.make_async_copy(zh_ref, zh, sem_z.at[0]), pltpu.make_async_copy(zl_ref, zl, sem_z.at[1])]
    passed = [pltpu.make_async_copy(l_ref, l, sem_l.at[0]), pltpu.make_async_copy(x_ref, x, sem_l.at[1])]
    passed_on = [pltpu.make_async_copy(l, lo_ref, sem_l.at[2]), pltpu.make_async_copy(x, xo_ref, sem_l.at[3])]
    outputs = []
    for copy in factors:
        copy.start()
    for i in range(AHEAD):
        for copy in inputs(i):
            copy.start()
    for copy in factors:
        copy.wait()
    for i in range(steps):
        if i + AHEAD < steps:
            for copy in inputs(i + AHEAD):
                copy.start()
        if i + AHEAD == steps:
            for copy in passed:
                copy.start()
        for copy in inputs(i):
            copy.wait()
        base = i * UNIT * cols
        kept = [keep_ref[base + k] for k in range(UNIT * cols)]
        many = sum(kept) > UNIT * cols // 2

        @pl.when(many)
        def _():
            rows = slice(i * size, (i + 1) * size)
            for j in range(cols):
                part = slice(j * BLOCK, (j + 1) * BLOCK)
                d = dot3((yh[rows, :], yl[rows, :]), (zh[part, :], zl[part, :]), NT)
                for r in range(UNIT):
                    at = slice(i * size + r * BLOCK, i * size + (r + 1) * BLOCK)
                    t[at, part] -= jnp.where(kept[r * cols + j] != 0, d[r * BLOCK:(r + 1) * BLOCK], 0.0)

        @pl.when(jnp.logical_not(many))
        def _():
            def block(k, carry):
                rows = pl.ds(pl.multiple_of(i * size + k // cols * BLOCK, BLOCK), BLOCK)
                part = pl.ds(pl.multiple_of(k % cols * BLOCK, BLOCK), BLOCK)

                @pl.when(keep_ref[base + k] != 0)
                def _():
                    t[rows, part] -= dot3((yh[rows, :], yl[rows, :]), (zh[part, :], zl[part, :]), NT)
                return carry
            lax.fori_loop(0, UNIT * cols, block, 0)
        rows = slice(i * size, (i + 1) * size)
        outputs.append(pltpu.make_async_copy(t.at[rows], o_ref.at[rows], sem_out.at[i]))
        outputs[-1].start()
        if i == steps - 2:
            for copy in passed:
                copy.wait()
            for copy in passed_on:
                copy.start()
    for copy in outputs + passed_on:
        copy.wait()


def update(keep, yh, yl, zh, zl, trailing, diag_factor, panel_factor):
    f32, bf = jnp.float32, jnp.bfloat16
    m, n = trailing.shape
    steps = m // (UNIT * BLOCK)
    anywhere, hbm = pl.BlockSpec(memory_space=pl.ANY), pl.BlockSpec(memory_space=pl.ANY)
    dma = pltpu.SemaphoreType.DMA
    return pl.pallas_call(
        update_kernel,
        out_shape=(jax.ShapeDtypeStruct((m, n), f32), jax.ShapeDtypeStruct(diag_factor.shape, f32),
                   jax.ShapeDtypeStruct(panel_factor.shape, f32)),
        in_specs=[pl.BlockSpec(memory_space=pltpu.SMEM), hbm, hbm, anywhere, anywhere, hbm, anywhere, anywhere],
        out_specs=(hbm,) * 3,
        scratch_shapes=[
            pltpu.VMEM(yh.shape, bf), pltpu.VMEM(yl.shape, bf), pltpu.VMEM(zh.shape, bf), pltpu.VMEM(zl.shape, bf),
            pltpu.VMEM((m, n), f32), pltpu.VMEM(diag_factor.shape, f32), pltpu.VMEM(panel_factor.shape, f32),
            dma((2,)), dma((steps, 3)), dma((steps,)), dma((4,)),
        ],
        compiler_params=pltpu.CompilerParams(vmem_limit_bytes=60 << 20),
        name="update",
    )(keep, yh, yl, zh, zl, trailing, diag_factor, panel_factor)


def local(front_diag, panel_rows, trailing, pattern):
    row_blocks, col_blocks = pattern.shape
    row_index = lax.axis_index("row") * row_blocks + jnp.arange(row_blocks)
    col_index = lax.axis_index("col") * col_blocks + jnp.arange(col_blocks)
    keep = pattern * (row_index[:, None] >= col_index[None, :]).astype(jnp.int32)
    diag_factor, panel_factor, yh, yl, zh, zl, _ = factor(front_diag, panel_rows, trailing.shape[1])
    schur, diag_factor, panel_factor = update(keep.reshape(-1), yh, yl, zh, zl, trailing, diag_factor, panel_factor)
    return (diag_factor, panel_factor, schur)


def solution(mesh):
    return jax.shard_map(
        local,
        mesh=mesh,
        in_specs=(P(), P(("row", "col"), None), P("row", "col"), P("row", "col")),
        out_specs=(P(), P(("row", "col"), None), P("row", "col")),
        check_vma=False,
    )
```

```python
import jax
import jax.numpy as jnp
from jax import lax
from jax.experimental import pallas as pl
from jax.experimental.pallas import tpu as pltpu
from jax.sharding import PartitionSpec as P

BLOCK = 256
SIDE = 4
GROUP = 512
HI = lax.Precision.HIGHEST
MESH = pl.DeviceIdType.MESH

NT = (((1,), (1,)), ((), ()))
NN = (((1,), (0,)), ((), ()))


def halves(x):
    high = x.astype(jnp.bfloat16)
    return high, (x - high.astype(jnp.float32)).astype(jnp.bfloat16)


def dot3(a, b, dims):
    def one(x, y):
        return lax.dot_general(x, y, dims, preferred_element_type=jnp.float32)
    return one(a[0], b[0]) + (one(a[0], b[1]) + one(a[1], b[0]))


def factor_tile(s, t):
    sub = lax.broadcasted_iota(jnp.int32, (8, 128), 0)
    def wide(x, c):
        return jnp.broadcast_to(x[:, c:c + 1], (8, 128))
    def tall(x, k):
        return jnp.broadcast_to(x[k:k + 1, :], (8, 128))
    n = len(s)
    for g in range(n):
        r, q = s[g], t[g]
        c = [wide(r, 8 * g + m) for m in range(8)]
        u = jnp.zeros((8, 128), jnp.float32)
        w = u
        for k in range(8):
            here = sub == k
            f = c[k]
            p = tall(f, k)
            inv = 1.0 / p
            root = lax.rsqrt(p)
            rk, qk = tall(r, k), tall(q, k)
            u = jnp.where(here, rk * root, u)
            w = jnp.where(here, qk * root, w)
            r = jnp.where(here, rk * inv, r - (f * rk) * inv)
            q = jnp.where(here, qk * inv, q - (f * qk) * inv)
            for m in range(k + 1, 8):
                cm = tall(c[m], k)
                c[m] = jnp.where(here, cm * inv, c[m] - (f * cm) * inv)
        for h in range(g + 1, n):
            sh, th = s[h], t[h]
            ds, dt = None, None
            for m in range(8):
                b = wide(s[h], 8 * g + m)
                a1, a2 = b * tall(r, m), b * tall(q, m)
                ds = a1 if ds is None else ds + a1
                dt = a2 if dt is None else dt + a2
            s[h], t[h] = sh - ds, th - dt
        s[g], t[g] = u, w
    return s, t


def thirds(x):
    f32 = jnp.float32
    h = x.astype(jnp.bfloat16)
    r = x - h.astype(f32)
    m = r.astype(jnp.bfloat16)
    return h, m, (r - m.astype(f32)).astype(jnp.bfloat16)

def wide_left(x):
    h, m, l = thirds(x)
    return jnp.concatenate([h, h, m, m, h, l], axis=1)

def tall_right(x):
    h, m, l = thirds(x)
    return jnp.concatenate([h, m, h, m, l, h], axis=0)

def dot6(a, b):
    return jnp.dot(a, b, preferred_element_type=jnp.float32)


class Exchange:
    def __init__(self, own, rows, cols, sems):
        self.own, self.rows, self.cols = own, rows, cols
        self.row_send, self.row_recv, self.col_send, self.col_recv, self.pair_send, self.here = sems
        row, col = lax.axis_index("row"), lax.axis_index("col")
        self.z, self.k, self.y, self.x = row // 2, row % 2, col // SIDE, col % SIDE
        self.piece = own.shape[0]
        self.half = self.piece // 2
        self.quarter = self.piece // 4

    def device(self, dx=0, dy=0, dz=0, dk=0):
        z, k = lax.rem(self.z + dz + SIDE, SIDE), lax.rem(self.k + dk, 2)
        y, x = lax.rem(self.y + dy + SIDE, SIDE), lax.rem(self.x + dx + SIDE, SIDE)
        return (z * 2 + k, y * SIDE + x)

    def greet(self):
        near = [self.device(dx=1), self.device(dx=-1), self.device(dy=1), self.device(dy=-1),
                self.device(dz=1), self.device(dz=-1), self.device(dk=1)]
        barrier = pltpu.get_barrier_semaphore()
        for device in near:
            pl.semaphore_signal(barrier, inc=1, device_id=device, device_id_type=MESH)
        pl.semaphore_wait(barrier, len(near))

    def origin(self, h, a, b):
        dx, dy = (a, b) if h == 0 else (b, a)
        return lax.rem(self.x + dx, SIDE), lax.rem(self.y + dy, SIDE)

    def row_slot(self, h, a, b, q=None):
        x, y = self.origin(h, a, b)
        start = (y * SIDE + x) * self.piece + h * self.half
        if q is None:
            return self.rows.at[pl.ds(pl.multiple_of(start, self.quarter), self.half)]
        return self.rows.at[pl.ds(pl.multiple_of(start + q * self.quarter, self.quarter), self.quarter)]

    def own_half(self, h):
        return self.own.at[pl.ds(h * self.half, self.half)]

    def row_copy(self, h, a, b, q, along, sign):
        to_a = (a - sign) % SIDE if along == 0 else a
        to_b = (b - sign) % SIDE if along == 1 else b
        index = ((h * SIDE + to_a) * SIDE + to_b) * 2 + (q or 0)
        slot = self.row_slot(h, a, b, q)
        src = self.own_half(h) if (a, b) == (0, 0) else slot
        on_x = (along == 0) == (h == 0)
        device = self.device(dx=sign) if on_x else self.device(dy=sign)
        return pltpu.make_async_remote_copy(
            src_ref=src, dst_ref=slot, send_sem=self.row_send.at[index], recv_sem=self.row_recv.at[index],
            device_id=device, device_id_type=MESH)

    def row_wait(self, h, a, b, q=None):
        index = ((h * SIDE + a) * SIDE + b) * 2 + (q or 0)
        slot = self.row_slot(h, a, b, q)
        pltpu.make_async_copy(slot, slot, self.row_recv.at[index]).wait()

    def sends(self):
        out = []
        for h in (0, 1):
            for sign in (1, -1):
                out.append((0, h, 0, 0, None, 0, sign))
        for h in (0, 1):
            for sign in (1, -1):
                out.append((0, h, 0, 0, None, 1, sign))
        for h in (0, 1):
            out += [(1, h, 3, 0, 0, 0, 1), (1, h, 1, 0, 1, 0, -1)]
        for h in (0, 1):
            for a in (1, 3):
                for sign in (1, -1):
                    out.append((1, h, a, 0, None, 1, sign))
        for h in (0, 1):
            for sign in (1, -1):
                out.append((2, h, 2, 0, None, 1, sign))
        for wave, places in ((2, (0,)), (3, (1, 3)), (4, (2,))):
            for h in (0, 1):
                for a in places:
                    out += [(wave, h, a, 3, 0, 1, 1), (wave, h, a, 1, 1, 1, -1)]
        return out

    ARRIVALS = (
        (),
        ((1, 0), (3, 0)),
        ((2, 0), (0, 1), (0, 3)),
        ((1, 1), (1, 3), (3, 1), (3, 3)),
        ((2, 1), (2, 3), (0, 2)),
        ((1, 2), (3, 2)),
        ((2, 2),),
    )

    def col_slot(self, h, a, b):
        x, y = self.origin(h, a, b)
        start = (lax.rem(y, 2) * SIDE + x) * self.piece + h * self.half
        return self.cols.at[pl.ds(pl.multiple_of(start, self.half), self.half)]

    def col_index(self, h, a, b):
        return (h * SIDE + a) * SIDE + b

    def in_cols(self, h, a, b):
        _, y = self.origin(h, a, b)
        return y // 2 == lax.rem(self.x, 2)

    def holder(self):
        return self.k == self.x // 2

    def at_hop(self, h, hop):
        if h == 0:
            return self.z - self.y == hop
        return (lax.rem(self.y - self.z + SIDE, SIDE) == hop) & (self.y < SIDE - 1)

    def goes_on(self, h):
        if h == 0:
            return (self.z >= self.y) & (self.z < SIDE - 1)
        return (lax.rem(self.y - self.z + SIDE, SIDE) < SIDE - 1) & (self.y < SIDE - 1)

    def needed(self):
        return self.z >= self.y

    def col_source(self, h, a, b, first):
        if not first:
            return self.col_slot(h, a, b)
        return self.own_half(h) if (a, b) == (0, 0) else self.row_slot(h, a, b)

    def along(self, h, a, b, first):
        index = self.col_index(h, a, b)
        return pltpu.make_async_remote_copy(
            src_ref=self.col_source(h, a, b, first), dst_ref=self.col_slot(h, a, b),
            send_sem=self.col_send.at[index], recv_sem=self.col_recv.at[index],
            device_id=self.device(dz=1 if h == 0 else -1), device_id_type=MESH)

    def across(self, h, a, b, first):
        index = self.col_index(h, a, b)
        return pltpu.make_async_remote_copy(
            src_ref=self.col_source(h, a, b, first), dst_ref=self.col_slot(h, a, b),
            send_sem=self.pair_send.at[index], recv_sem=self.col_recv.at[index],
            device_id=self.device(dk=1), device_id_type=MESH)

    def keep_copy(self, h, a, b):
        src = self.col_source(h, a, b, True)
        return pltpu.make_async_copy(src, self.col_slot(h, a, b), self.here.at[self.col_index(h, a, b)])

    def col_wait(self, h, a, b):
        slot = self.col_slot(h, a, b)
        pltpu.make_async_copy(slot, slot, self.col_recv.at[self.col_index(h, a, b)]).wait()

    def pieces(self, wave):
        return [(h, a, b) for h in (0, 1) for a, b in (((0, 0),) if wave == 0 else self.ARRIVALS[wave])]

    def start_rows(self, wave):
        for h in (0, 1):
            for a, b in self.ARRIVALS[wave]:
                if b == 2 or (a == 2 and b == 0):
                    self.row_wait(h, a, b, 0)
                    self.row_wait(h, a, b, 1)
                else:
                    self.row_wait(h, a, b)
        for entry in self.sends():
            if entry[0] == wave:
                self.row_copy(*entry[1:]).start()

    def start_cols(self, wave):
        for h, a, b in self.pieces(wave):
            inside = self.in_cols(h, a, b) & self.holder() & (self.z == self.y)

            @pl.when(inside)
            def _():
                self.across(h, a, b, True).start()
                self.keep_copy(h, a, b).start()

            @pl.when(inside & (self.z < SIDE - 1))
            def _():
                self.along(h, a, b, True).start()

    def relay_cols(self, h, a, b, hop):
        here = self.in_cols(h, a, b) & self.holder() & self.at_hop(h, hop)

        @pl.when(here)
        def _():
            self.col_wait(h, a, b)

        @pl.when(here & self.goes_on(h))
        def _():
            self.along(h, a, b, False).start()

        @pl.when(here & self.needed())
        def _():
            self.across(h, a, b, False).start()

    def own_row(self):
        return self.y // 2 == lax.rem(self.x, 2)

    def early_half(self):
        return jnp.where(self.own_row(), lax.rem(self.y, 2), 1 - lax.rem(self.y, 2))

    def finish_cols(self, early):
        for wave in range(len(self.ARRIVALS)):
            for h, a, b in self.pieces(wave):
                dy = b if h == 0 else a
                if dy == (2 if early else 0):
                    continue
                inside = self.in_cols(h, a, b) & self.needed()
                if dy % 2 == 1:
                    inside = inside & (jnp.logical_not(self.own_row()) if early else self.own_row())

                @pl.when(inside & self.holder() & (self.z == self.y))
                def _():
                    self.keep_copy(h, a, b).wait()

                @pl.when(inside & jnp.logical_not(self.holder()))
                def _():
                    self.col_wait(h, a, b)

    def finish(self):
        for entry in self.sends():
            self.row_copy(*entry[1:]).wait_send()
        for wave in range(len(self.ARRIVALS)):
            for h, a, b in self.pieces(wave):
                inside = self.in_cols(h, a, b) & self.holder()

                @pl.when(inside & self.needed())
                def _():
                    self.across(h, a, b, False).wait_send()

                @pl.when(inside & self.goes_on(h))
                def _():
                    self.along(h, a, b, False).wait_send()


ROW_POINTS = (0, 1, 3, 5, 6, 7, 8)
STEPS = 4
POINTS = [0.0] + [2.5 + 5.6 * (k + 1) for k in range(8)] + [49.5 + 0.65 * i for i in range(16)] + [60.5 + 0.7 * i for i in range(40)]


def relay_points():
    table = {}
    for kind in ((0, 1), (2, 3), (3, 0), (1, 2)):
        for h in (0, 1):
            free = [0.0] * (SIDE - 1)
            for wave, places in enumerate(Exchange.ARRIVALS):
                for a, b in (((0, 0),) if wave == 0 else places):
                    if (b if h == 0 else a) not in kind:
                        continue
                    ready = POINTS[ROW_POINTS[wave]]
                    for hop in range(1, SIDE):
                        free[hop - 1] = max(ready, free[hop - 1]) + 2.8
                        arrival = free[hop - 1] + 1.8
                        point = min([i for i, t in enumerate(POINTS) if t >= arrival], default=len(POINTS) - 1)
                        ready = POINTS[point]
                        table[h, a, b, hop] = max(point, table.get((h, a, b, hop), 0))
    return table


RELAYS = relay_points()


def transfers(exchange, point, near=False, far=False):
    for wave, at in enumerate(ROW_POINTS):
        if at == point:
            exchange.start_rows(wave)
            exchange.start_cols(wave)
    for (h, a, b, hop), at in RELAYS.items():
        if at == point and not (near and (a, b) == (2, 2)) and not (far and (a, b) != (2, 2)):
            exchange.relay_cols(h, a, b, hop)


def factor_kernel(a_ref, own_in, l_out, x_ref, yh_ref, yl_ref, zh_ref, zl_ref, rows_ref,
                  w_ref, l_ref, g_ref, d_ref, u_ref, wd_ref, cols_ref, wh, wl, r_buf, zf, rh, rl, yh_buf, yl_buf,
                  ch, cl, zh_buf, zl_buf, own_ref, sem_a, sem_own, sem_l, sem_in, sem_out, sem_z, *sems):
    n = a_ref.shape[0]
    nb = n // 128
    load_own = pltpu.make_async_copy(own_in, own_ref, sem_own)
    load_own.start()
    load = pltpu.make_async_copy(a_ref, w_ref, sem_a)
    load.start()
    exchange = Exchange(own_ref, rows_ref, cols_ref, sems)
    l_ref[...] = jnp.zeros_like(l_ref)
    wd_ref[...] = jnp.zeros_like(wd_ref)
    u_ref[...] = jnp.zeros_like(u_ref)
    exchange.greet()
    load_own.wait()
    me = lax.axis_index("col")
    first = pl.multiple_of(me * own_ref.shape[0], own_ref.shape[0])
    keep_own = pltpu.make_async_copy(own_ref, rows_ref.at[pl.ds(first, own_ref.shape[0])], sem_own)
    transfers(exchange, 0)
    keep_own.start()
    load.wait()
    d_ref[...] = w_ref[:128, :128]
    sub = lax.broadcasted_iota(jnp.int32, (8, 128), 0)
    lane = lax.broadcasted_iota(jnp.int32, (8, 128), 1)
    lane_all = lax.broadcasted_iota(jnp.int32, (128, n), 1)

    def settle(p, last):
        q = jnp.maximum(p - 1, 0)
        oq = pl.multiple_of(q * 128, 128)
        wd = wd_ref[...]
        row = w_ref[pl.ds(oq, 128), :]
        g = dot6(wide_left(wd), tall_right(row))
        inside = (lane_all >= oq) & (lane_all < oq + 128)
        done = jnp.where(lane_all < oq, g, 0.0)
        w_ref[pl.ds(oq, 128), :] = done if last else jnp.where(p > 0, done, row)
        l_ref[pl.ds(oq, 128), pl.ds(oq, 128)] = u_ref[...].T
        if last:
            w_ref[pl.ds(oq, 128), pl.ds(oq, 128)] = wd
            wh[pl.ds(oq, 128), :], wl[pl.ds(oq, 128), :] = halves(w_ref[pl.ds(oq, 128), :])
            return
        g_ref[...] = g
        g_ref[:, pl.ds(oq, 128)] += wd
        right = tall_right(g_ref[...])
        for i in range(1, nb):
            li = jnp.where(q < i, g[:, i * 128:(i + 1) * 128], 0.0).T
            l_ref[i * 128:(i + 1) * 128, pl.ds(oq, 128)] = jnp.where(q < i, li, l_ref[i * 128:(i + 1) * 128, pl.ds(oq, 128)])
            w_ref[i * 128:(i + 1) * 128, :] -= dot6(wide_left(li), right)
        w_ref[pl.ds(oq, 128), pl.ds(oq, 128)] = jnp.where(p > 0, wd, w_ref[pl.ds(oq, 128), pl.ds(oq, 128)])
        wh[pl.ds(oq, 128), :], wl[pl.ds(oq, 128), :] = halves(done)
        wh[pl.ds(oq, 128), pl.ds(oq, 128)], wl[pl.ds(oq, 128), pl.ds(oq, 128)] = halves(wd)

    def panel(p, carry):
        o = pl.multiple_of(p * 128, 128)
        o1 = pl.multiple_of(jnp.minimum(p + 1, nb - 1) * 128, 128)
        s = [d_ref[8 * g:8 * g + 8, :] for g in range(16)]
        t = [(lane == sub + 8 * g).astype(jnp.float32) for g in range(16)]
        s, t = factor_tile(s, t)
        settle(p, False)
        for g in range(16):
            u_ref[8 * g:8 * g + 8, :] = jnp.where(lane >= sub + 8 * g, s[g], 0.0)
            wd_ref[8 * g:8 * g + 8, :] = t[g]
        un = dot6(wide_left(wd_ref[...]), tall_right(w_ref[pl.ds(o, 128), pl.ds(o1, 128)]))
        d_ref[...] = w_ref[pl.ds(o1, 128), pl.ds(o1, 128)] - dot6(wide_left(un.T), tall_right(un))
        for k in range(nb):
            @pl.when(p == k)
            def _():
                transfers(exchange, k + 1)
        return carry
    lax.fori_loop(0, nb, panel, 0)
    keep_own.wait()

    def fetch(b, slot):
        rows = rows_ref.at[pl.ds(pl.multiple_of(b * GROUP, GROUP), GROUP)]
        return pltpu.make_async_copy(rows, r_buf.at[slot], sem_in.at[slot])

    def store(b, slot):
        part = pl.ds(pl.multiple_of(b * GROUP, GROUP), GROUP)
        return (pltpu.make_async_copy(yh_buf.at[slot], yh_ref.at[part], sem_out.at[slot, 0]),
                pltpu.make_async_copy(yl_buf.at[slot], yl_ref.at[part], sem_out.at[slot, 1]))

    blocks = rows_ref.shape[0] // GROUP
    fetch(0, 0).start()
    settle(nb, True)
    save_l = pltpu.make_async_copy(l_ref, l_out, sem_l)
    save_l.start()

    def passing(b, j):
        for k in range(blocks):
            at = nb + 1 + STEPS * k + j
            if at in RELAYS.values():
                @pl.when(b == k)
                def _():
                    transfers(exchange, at)

    def transform(b, carry):
        slot = lax.rem(b, 2)
        fetch(b, slot).wait()

        @pl.when(b + 1 < blocks)
        def _():
            fetch(b + 1, 1 - slot).start()

        @pl.when(b >= 2)
        def _():
            for copy in store(b - 2, slot):
                copy.wait()
        rh[...], rl[...] = halves(r_buf[slot])
        for j, p in enumerate(range(0, n, BLOCK)):
            e = p + BLOCK
            z = dot3((rh[:, :e], rl[:, :e]), (wh[p:e, :e], wl[p:e, :e]), NT)
            zf[:, p:e] = z
            yh_buf[slot, :, p:e], yl_buf[slot, :, p:e] = halves(z)
            passing(b, j)
        for copy in store(b, slot):
            copy.start()
        per = GROUP // own_ref.shape[0]

        @pl.when(me // per == b)
        def _():
            x_ref[...] = zf[pl.ds(pl.multiple_of(lax.rem(me, per) * own_ref.shape[0], own_ref.shape[0]), own_ref.shape[0]), :]
        return carry
    lax.fori_loop(0, blocks, transform, 0)
    late = sorted({at for (h, a, b, hop), at in RELAYS.items() if (a, b) == (2, 2) and at >= nb + 1 + STEPS * blocks})
    for point in range(nb + 1 + STEPS * blocks, len(POINTS)):
        transfers(exchange, point, near=True)
    saves = []
    size = cols_ref.shape[0] // 2

    def column_factor(early):
        exchange.finish_cols(early)
        half = exchange.early_half() if early else 1 - exchange.early_half()
        part = pl.ds(pl.multiple_of(half * size, size), size)
        ch[...], cl[...] = halves(cols_ref[part, :])
        for j, p in enumerate(range(0, n, BLOCK)):
            e = p + BLOCK
            z = dot3((ch[:, :e], cl[:, :e]), (wh[p:e, :e], wl[p:e, :e]), NT)
            zh_buf[part, p:e], zl_buf[part, p:e] = halves(z)
            for k, (a, b) in enumerate(((zh_buf, zh_ref), (zl_buf, zl_ref))):
                saves.append(pltpu.make_async_copy(a.at[part, p:e], b.at[part, p:e], sem_z.at[int(early), j, k]))
                saves[-1].start()
            if early and j % 2 == 1 and late:
                transfers(exchange, late.pop(0), far=True)
    column_factor(True)
    for point in late:
        transfers(exchange, point, far=True)
    column_factor(False)
    exchange.finish()
    for b in (blocks - 2, blocks - 1):
        for copy in store(b, b % 2):
            copy.wait()
    for copy in [save_l] + saves:
        copy.wait()


def factor(front_diag, own, cols):
    f32, bf = jnp.float32, jnp.bfloat16
    n = front_diag.shape[0]
    rows = lax.axis_size("col") * own.shape[0]
    vm, anywhere = pl.BlockSpec(memory_space=pltpu.VMEM), pl.BlockSpec(memory_space=pl.ANY)
    hbm = pl.BlockSpec(memory_space=pl.ANY)
    dma = pltpu.SemaphoreType.DMA
    return pl.pallas_call(
        factor_kernel,
        out_shape=(
            jax.ShapeDtypeStruct((n, n), f32),
            jax.ShapeDtypeStruct(own.shape, f32),
            jax.ShapeDtypeStruct((rows, n), bf),
            jax.ShapeDtypeStruct((rows, n), bf),
            jax.ShapeDtypeStruct((cols, n), bf),
            jax.ShapeDtypeStruct((cols, n), bf),
            jax.ShapeDtypeStruct((rows, n), f32),
        ),
        in_specs=[hbm, hbm],
        out_specs=(anywhere, vm, hbm, hbm, anywhere, anywhere, hbm),
        scratch_shapes=[
            pltpu.VMEM((n, n), f32), pltpu.VMEM((n, n), f32), pltpu.VMEM((128, n), f32),
            pltpu.VMEM((128, 128), f32), pltpu.VMEM((128, 128), f32), pltpu.VMEM((128, 128), f32),
            pltpu.VMEM((cols, n), f32),
            pltpu.VMEM((n, n), bf), pltpu.VMEM((n, n), bf),
            pltpu.VMEM((2, GROUP, n), f32), pltpu.VMEM((GROUP, n), f32),
            pltpu.VMEM((GROUP, n), bf), pltpu.VMEM((GROUP, n), bf),
            pltpu.VMEM((2, GROUP, n), bf), pltpu.VMEM((2, GROUP, n), bf),
            pltpu.VMEM((cols // 2, n), bf), pltpu.VMEM((cols // 2, n), bf),
            pltpu.VMEM((cols, n), bf), pltpu.VMEM((cols, n), bf),
            pltpu.VMEM(own.shape, f32),
            dma, dma, dma, dma((2,)), dma((2, 2)), dma((2, n // BLOCK, 2)),
            dma((64,)), dma((64,)), dma((32,)), dma((32,)), dma((32,)), dma((32,)),
        ],
        compiler_params=pltpu.CompilerParams(vmem_limit_bytes=56 << 20, collective_id=0, has_side_effects=True),
        name="factor",
    )(front_diag, own)


UNIT = 2
AHEAD = 2


def update_kernel(pattern_ref, yh_ref, yl_ref, zh_ref, zl_ref, t_ref, l_ref, x_ref, o_ref, lo_ref, xo_ref,
                  yh, yl, zh, zl, t, l, x, sem_z, sem_in, sem_out, sem_l):
    n = t.shape[1]
    size = UNIT * BLOCK
    steps, cols = t.shape[0] // size, n // BLOCK
    first_row = lax.axis_index("row") * (steps * UNIT)
    first_col = lax.axis_index("col") * cols

    def keep(r, c):
        return (pattern_ref[c, r] != 0) & (first_row + r >= first_col + c)

    def inputs(i):
        part = slice(i * size, (i + 1) * size)
        return [pltpu.make_async_copy(a.at[part], b.at[part], sem_in.at[i, k])
                for k, (a, b) in enumerate(((yh_ref, yh), (yl_ref, yl), (t_ref, t)))]
    factors = [pltpu.make_async_copy(zh_ref, zh, sem_z.at[0]), pltpu.make_async_copy(zl_ref, zl, sem_z.at[1])]
    passed = [pltpu.make_async_copy(l_ref, l, sem_l.at[0]), pltpu.make_async_copy(x_ref, x, sem_l.at[1])]
    passed_on = [pltpu.make_async_copy(l, lo_ref, sem_l.at[2]), pltpu.make_async_copy(x, xo_ref, sem_l.at[3])]
    outputs = []
    for copy in factors:
        copy.start()
    for i in range(AHEAD):
        for copy in inputs(i):
            copy.start()
    for copy in factors:
        copy.wait()
    for i in range(steps):
        if i + AHEAD < steps:
            for copy in inputs(i + AHEAD):
                copy.start()
        if i + AHEAD == steps:
            for copy in passed:
                copy.start()
        for copy in inputs(i):
            copy.wait()
        kept = [keep(i * UNIT + k // cols, k % cols) for k in range(UNIT * cols)]
        many = sum(k.astype(jnp.int32) for k in kept) > UNIT * cols // 2

        @pl.when(many)
        def _():
            rows = slice(i * size, (i + 1) * size)
            for j in range(cols):
                part = slice(j * BLOCK, (j + 1) * BLOCK)
                d = dot3((yh[rows, :], yl[rows, :]), (zh[part, :], zl[part, :]), NT)
                for r in range(UNIT):
                    at = slice(i * size + r * BLOCK, i * size + (r + 1) * BLOCK)
                    t[at, part] -= jnp.where(kept[r * cols + j], d[r * BLOCK:(r + 1) * BLOCK], 0.0)

        @pl.when(jnp.logical_not(many))
        def _():
            def block(k, carry):
                rows = pl.ds(pl.multiple_of(i * size + k // cols * BLOCK, BLOCK), BLOCK)
                part = pl.ds(pl.multiple_of(k % cols * BLOCK, BLOCK), BLOCK)

                @pl.when(keep(i * UNIT + k // cols, k % cols))
                def _():
                    t[rows, part] -= dot3((yh[rows, :], yl[rows, :]), (zh[part, :], zl[part, :]), NT)
                return carry
            lax.fori_loop(0, UNIT * cols, block, 0)
        rows = slice(i * size, (i + 1) * size)
        outputs.append(pltpu.make_async_copy(t.at[rows], o_ref.at[rows], sem_out.at[i]))
        outputs[-1].start()
        if i == steps - 2:
            for copy in passed:
                copy.wait()
            for copy in passed_on:
                copy.start()
    for copy in outputs + passed_on:
        copy.wait()


def update(pattern, yh, yl, zh, zl, trailing, diag_factor, panel_factor):
    f32, bf = jnp.float32, jnp.bfloat16
    m, n = trailing.shape
    steps = m // (UNIT * BLOCK)
    anywhere, hbm = pl.BlockSpec(memory_space=pl.ANY), pl.BlockSpec(memory_space=pl.ANY)
    dma = pltpu.SemaphoreType.DMA
    return pl.pallas_call(
        update_kernel,
        out_shape=(jax.ShapeDtypeStruct((m, n), f32), jax.ShapeDtypeStruct(diag_factor.shape, f32),
                   jax.ShapeDtypeStruct(panel_factor.shape, f32)),
        in_specs=[pl.BlockSpec(memory_space=pltpu.SMEM), hbm, hbm, anywhere, anywhere, hbm, anywhere, anywhere],
        out_specs=(hbm,) * 3,
        scratch_shapes=[
            pltpu.VMEM(yh.shape, bf), pltpu.VMEM(yl.shape, bf), pltpu.VMEM(zh.shape, bf), pltpu.VMEM(zl.shape, bf),
            pltpu.VMEM((m, n), f32), pltpu.VMEM(diag_factor.shape, f32), pltpu.VMEM(panel_factor.shape, f32),
            dma((2,)), dma((steps, 3)), dma((steps,)), dma((4,)),
        ],
        compiler_params=pltpu.CompilerParams(vmem_limit_bytes=60 << 20),
        name="update",
    )(pattern, yh, yl, zh, zl, trailing, diag_factor, panel_factor)


def local(front_diag, panel_rows, trailing, pattern):
    diag_factor, panel_factor, yh, yl, zh, zl, _ = factor(front_diag, panel_rows, trailing.shape[1])
    schur, diag_factor, panel_factor = update(pattern.T, yh, yl, zh, zl, trailing, diag_factor, panel_factor)
    return (diag_factor, panel_factor, schur)


def solution(mesh):
    return jax.shard_map(
        local,
        mesh=mesh,
        in_specs=(P(), P(("row", "col"), None), P("row", "col"), P("row", "col")),
        out_specs=(P(), P(("row", "col"), None), P("row", "col")),
        check_vma=False,
    )
```

```python
import jax
import jax.numpy as jnp
from jax import lax
from jax.experimental import pallas as pl
from jax.experimental.pallas import tpu as pltpu
from jax.sharding import PartitionSpec as P

BLOCK = 256
SIDE = 4
GROUP = 512
HI = lax.Precision.HIGHEST
MESH = pl.DeviceIdType.MESH

NT = (((1,), (1,)), ((), ()))
NN = (((1,), (0,)), ((), ()))


def halves(x):
    high = x.astype(jnp.bfloat16)
    return high, (x - high.astype(jnp.float32)).astype(jnp.bfloat16)


def dot3(a, b, dims):
    def one(x, y):
        return lax.dot_general(x, y, dims, preferred_element_type=jnp.float32)
    return one(a[0], b[0]) + (one(a[0], b[1]) + one(a[1], b[0]))


def factor_tile(s, t):
    sub = lax.broadcasted_iota(jnp.int32, (8, 128), 0)
    def wide(x, c):
        return jnp.broadcast_to(x[:, c:c + 1], (8, 128))
    def tall(x, k):
        return jnp.broadcast_to(x[k:k + 1, :], (8, 128))
    n = len(s)
    for g in range(n):
        r, q = s[g], t[g]
        c = [wide(r, 8 * g + m) for m in range(8)]
        u = jnp.zeros((8, 128), jnp.float32)
        w = u
        for k in range(8):
            here = sub == k
            f = c[k]
            p = tall(f, k)
            inv = 1.0 / p
            root = lax.rsqrt(p)
            rk, qk = tall(r, k), tall(q, k)
            u = jnp.where(here, rk * root, u)
            w = jnp.where(here, qk * root, w)
            r = jnp.where(here, rk * inv, r - (f * rk) * inv)
            q = jnp.where(here, qk * inv, q - (f * qk) * inv)
            for m in range(k + 1, 8):
                cm = tall(c[m], k)
                c[m] = jnp.where(here, cm * inv, c[m] - (f * cm) * inv)
        for h in range(g + 1, n):
            sh, th = s[h], t[h]
            ds, dt = None, None
            for m in range(8):
                b = wide(s[h], 8 * g + m)
                a1, a2 = b * tall(r, m), b * tall(q, m)
                ds = a1 if ds is None else ds + a1
                dt = a2 if dt is None else dt + a2
            s[h], t[h] = sh - ds, th - dt
        s[g], t[g] = u, w
    return s, t


def thirds(x):
    f32 = jnp.float32
    h = x.astype(jnp.bfloat16)
    r = x - h.astype(f32)
    m = r.astype(jnp.bfloat16)
    return h, m, (r - m.astype(f32)).astype(jnp.bfloat16)

def wide_left(x):
    h, m, l = thirds(x)
    return jnp.concatenate([h, h, m, m, h, l], axis=1)

def tall_right(x):
    h, m, l = thirds(x)
    return jnp.concatenate([h, m, h, m, l, h], axis=0)

def dot6(a, b):
    return jnp.dot(a, b, preferred_element_type=jnp.float32)


class Exchange:
    def __init__(self, own, rows, cols, sems):
        self.own, self.rows, self.cols = own, rows, cols
        self.row_send, self.row_recv, self.col_send, self.col_recv, self.pair_send, self.here = sems
        row, col = lax.axis_index("row"), lax.axis_index("col")
        self.z, self.k, self.y, self.x = row // 2, row % 2, col // SIDE, col % SIDE
        self.piece = own.shape[0]
        self.half = self.piece // 2
        self.quarter = self.piece // 4

    def device(self, dx=0, dy=0, dz=0, dk=0):
        z, k = lax.rem(self.z + dz + SIDE, SIDE), lax.rem(self.k + dk, 2)
        y, x = lax.rem(self.y + dy + SIDE, SIDE), lax.rem(self.x + dx + SIDE, SIDE)
        return (z * 2 + k, y * SIDE + x)

    def greet(self):
        near = [self.device(dx=1), self.device(dx=-1), self.device(dy=1), self.device(dy=-1),
                self.device(dz=1), self.device(dz=-1), self.device(dk=1)]
        barrier = pltpu.get_barrier_semaphore()
        for device in near:
            pl.semaphore_signal(barrier, inc=1, device_id=device, device_id_type=MESH)
        pl.semaphore_wait(barrier, len(near))

    def origin(self, h, a, b):
        dx, dy = (a, b) if h == 0 else (b, a)
        return lax.rem(self.x + dx, SIDE), lax.rem(self.y + dy, SIDE)

    def row_slot(self, h, a, b, q=None):
        x, y = self.origin(h, a, b)
        start = (y * SIDE + x) * self.piece + h * self.half
        if q is None:
            return self.rows.at[pl.ds(pl.multiple_of(start, self.quarter), self.half)]
        return self.rows.at[pl.ds(pl.multiple_of(start + q * self.quarter, self.quarter), self.quarter)]

    def own_half(self, h):
        return self.own.at[pl.ds(h * self.half, self.half)]

    def row_copy(self, h, a, b, q, along, sign):
        to_a = (a - sign) % SIDE if along == 0 else a
        to_b = (b - sign) % SIDE if along == 1 else b
        index = ((h * SIDE + to_a) * SIDE + to_b) * 2 + (q or 0)
        slot = self.row_slot(h, a, b, q)
        src = self.own_half(h) if (a, b) == (0, 0) else slot
        on_x = (along == 0) == (h == 0)
        device = self.device(dx=sign) if on_x else self.device(dy=sign)
        return pltpu.make_async_remote_copy(
            src_ref=src, dst_ref=slot, send_sem=self.row_send.at[index], recv_sem=self.row_recv.at[index],
            device_id=device, device_id_type=MESH)

    def row_wait(self, h, a, b, q=None):
        index = ((h * SIDE + a) * SIDE + b) * 2 + (q or 0)
        slot = self.row_slot(h, a, b, q)
        pltpu.make_async_copy(slot, slot, self.row_recv.at[index]).wait()

    def sends(self):
        out = []
        for h in (0, 1):
            for sign in (1, -1):
                out.append((0, h, 0, 0, None, 0, sign))
        for h in (0, 1):
            for sign in (1, -1):
                out.append((0, h, 0, 0, None, 1, sign))
        for h in (0, 1):
            out += [(1, h, 3, 0, 0, 0, 1), (1, h, 1, 0, 1, 0, -1)]
        for h in (0, 1):
            for a in (1, 3):
                for sign in (1, -1):
                    out.append((1, h, a, 0, None, 1, sign))
        for h in (0, 1):
            for sign in (1, -1):
                out.append((2, h, 2, 0, None, 1, sign))
        for wave, places in ((2, (0,)), (3, (1, 3)), (4, (2,))):
            for h in (0, 1):
                for a in places:
                    out += [(wave, h, a, 3, 0, 1, 1), (wave, h, a, 1, 1, 1, -1)]
        return out

    ARRIVALS = (
        (),
        ((1, 0), (3, 0)),
        ((2, 0), (0, 1), (0, 3)),
        ((1, 1), (1, 3), (3, 1), (3, 3)),
        ((2, 1), (2, 3), (0, 2)),
        ((1, 2), (3, 2)),
        ((2, 2),),
    )

    def col_slot(self, h, a, b):
        x, y = self.origin(h, a, b)
        start = (lax.rem(y, 2) * SIDE + x) * self.piece + h * self.half
        return self.cols.at[pl.ds(pl.multiple_of(start, self.half), self.half)]

    def col_index(self, h, a, b):
        return (h * SIDE + a) * SIDE + b

    def in_cols(self, h, a, b):
        _, y = self.origin(h, a, b)
        return y // 2 == lax.rem(self.x, 2)

    def holder(self):
        return self.k == self.x // 2

    def at_hop(self, h, hop):
        if h == 0:
            return self.z - self.y == hop
        return (lax.rem(self.y - self.z + SIDE, SIDE) == hop) & (self.y < SIDE - 1)

    def goes_on(self, h):
        if h == 0:
            return (self.z >= self.y) & (self.z < SIDE - 1)
        return (lax.rem(self.y - self.z + SIDE, SIDE) < SIDE - 1) & (self.y < SIDE - 1)

    def needed(self):
        return self.z >= self.y

    def col_source(self, h, a, b, first):
        if not first:
            return self.col_slot(h, a, b)
        return self.own_half(h) if (a, b) == (0, 0) else self.row_slot(h, a, b)

    def along(self, h, a, b, first):
        index = self.col_index(h, a, b)
        return pltpu.make_async_remote_copy(
            src_ref=self.col_source(h, a, b, first), dst_ref=self.col_slot(h, a, b),
            send_sem=self.col_send.at[index], recv_sem=self.col_recv.at[index],
            device_id=self.device(dz=1 if h == 0 else -1), device_id_type=MESH)

    def across(self, h, a, b, first):
        index = self.col_index(h, a, b)
        return pltpu.make_async_remote_copy(
            src_ref=self.col_source(h, a, b, first), dst_ref=self.col_slot(h, a, b),
            send_sem=self.pair_send.at[index], recv_sem=self.col_recv.at[index],
            device_id=self.device(dk=1), device_id_type=MESH)

    def keep_copy(self, h, a, b):
        src = self.col_source(h, a, b, True)
        return pltpu.make_async_copy(src, self.col_slot(h, a, b), self.here.at[self.col_index(h, a, b)])

    def col_wait(self, h, a, b):
        slot = self.col_slot(h, a, b)
        pltpu.make_async_copy(slot, slot, self.col_recv.at[self.col_index(h, a, b)]).wait()

    def pieces(self, wave):
        return [(h, a, b) for h in (0, 1) for a, b in (((0, 0),) if wave == 0 else self.ARRIVALS[wave])]

    def start_rows(self, wave):
        for h in (0, 1):
            for a, b in self.ARRIVALS[wave]:
                if b == 2 or (a == 2 and b == 0):
                    self.row_wait(h, a, b, 0)
                    self.row_wait(h, a, b, 1)
                else:
                    self.row_wait(h, a, b)
        for entry in self.sends():
            if entry[0] == wave:
                self.row_copy(*entry[1:]).start()

    def start_cols(self, wave):
        for h, a, b in self.pieces(wave):
            inside = self.in_cols(h, a, b) & self.holder() & (self.z == self.y)

            @pl.when(inside)
            def _():
                self.across(h, a, b, True).start()
                self.keep_copy(h, a, b).start()

            @pl.when(inside & (self.z < SIDE - 1))
            def _():
                self.along(h, a, b, True).start()

    def relay_cols(self, h, a, b, hop):
        here = self.in_cols(h, a, b) & self.holder() & self.at_hop(h, hop)

        @pl.when(here)
        def _():
            self.col_wait(h, a, b)

        @pl.when(here & self.goes_on(h))
        def _():
            self.along(h, a, b, False).start()

        @pl.when(here & self.needed())
        def _():
            self.across(h, a, b, False).start()

    def own_row(self):
        return self.y // 2 == lax.rem(self.x, 2)

    def early_half(self):
        return jnp.where(self.own_row(), lax.rem(self.y, 2), 1 - lax.rem(self.y, 2))

    def finish_cols(self, early):
        for wave in range(len(self.ARRIVALS)):
            for h, a, b in self.pieces(wave):
                dy = b if h == 0 else a
                if dy == (2 if early else 0):
                    continue
                inside = self.in_cols(h, a, b) & self.needed()
                if dy % 2 == 1:
                    inside = inside & (jnp.logical_not(self.own_row()) if early else self.own_row())

                @pl.when(inside & self.holder() & (self.z == self.y))
                def _():
                    self.keep_copy(h, a, b).wait()

                @pl.when(inside & jnp.logical_not(self.holder()))
                def _():
                    self.col_wait(h, a, b)

    def finish(self):
        for entry in self.sends():
            self.row_copy(*entry[1:]).wait_send()
        for wave in range(len(self.ARRIVALS)):
            for h, a, b in self.pieces(wave):
                inside = self.in_cols(h, a, b) & self.holder()

                @pl.when(inside & self.needed())
                def _():
                    self.across(h, a, b, False).wait_send()

                @pl.when(inside & self.goes_on(h))
                def _():
                    self.along(h, a, b, False).wait_send()


ROW_POINTS = (0, 1, 3, 5, 6, 7, 8)
STEPS = 4
POINTS = [0.0] + [2.5 + 5.6 * (k + 1) for k in range(8)] + [49.5 + 0.65 * i for i in range(16)] + [60.5 + 0.7 * i for i in range(40)]


def relay_points():
    table = {}
    for kind in ((0, 1), (2, 3), (3, 0), (1, 2)):
        for h in (0, 1):
            free = [0.0] * (SIDE - 1)
            for wave, places in enumerate(Exchange.ARRIVALS):
                for a, b in (((0, 0),) if wave == 0 else places):
                    if (b if h == 0 else a) not in kind:
                        continue
                    ready = POINTS[ROW_POINTS[wave]]
                    for hop in range(1, SIDE):
                        free[hop - 1] = max(ready, free[hop - 1]) + 2.8
                        arrival = free[hop - 1] + 1.8
                        point = min([i for i, t in enumerate(POINTS) if t >= arrival], default=len(POINTS) - 1)
                        ready = POINTS[point]
                        table[h, a, b, hop] = max(point, table.get((h, a, b, hop), 0))
    return table


RELAYS = relay_points()


def transfers(exchange, point, near=False, far=False):
    for wave, at in enumerate(ROW_POINTS):
        if at == point:
            exchange.start_rows(wave)
            exchange.start_cols(wave)
    for (h, a, b, hop), at in RELAYS.items():
        if at == point and not (near and (a, b) == (2, 2)) and not (far and (a, b) != (2, 2)):
            exchange.relay_cols(h, a, b, hop)


def factor_kernel(a_ref, own_in, l_out, x_ref, yh_ref, yl_ref, zh_ref, zl_ref, rows_ref,
                  w_ref, l_ref, g_ref, d_ref, u_ref, wd_ref, cols_ref, wh, wl, r_buf, zf, rh, rl, yh_buf, yl_buf,
                  ch, cl, zh_buf, zl_buf, own_ref, sem_a, sem_own, sem_l, sem_in, sem_out, sem_z, *sems):
    n = a_ref.shape[0]
    nb = n // 128
    load_own = pltpu.make_async_copy(own_in, own_ref, sem_own)
    load_own.start()
    load = pltpu.make_async_copy(a_ref, w_ref, sem_a)
    load.start()
    exchange = Exchange(own_ref, rows_ref, cols_ref, sems)
    l_ref[...] = jnp.zeros_like(l_ref)
    wd_ref[...] = jnp.zeros_like(wd_ref)
    u_ref[...] = jnp.zeros_like(u_ref)
    exchange.greet()
    load_own.wait()
    me = lax.axis_index("col")
    first = pl.multiple_of(me * own_ref.shape[0], own_ref.shape[0])
    keep_own = pltpu.make_async_copy(own_ref, rows_ref.at[pl.ds(first, own_ref.shape[0])], sem_own)
    transfers(exchange, 0)
    keep_own.start()
    load.wait()
    d_ref[...] = w_ref[:128, :128]
    sub = lax.broadcasted_iota(jnp.int32, (8, 128), 0)
    lane = lax.broadcasted_iota(jnp.int32, (8, 128), 1)
    lane_all = lax.broadcasted_iota(jnp.int32, (128, n), 1)

    def settle(p, last):
        q = jnp.maximum(p - 1, 0)
        oq = pl.multiple_of(q * 128, 128)
        wd = wd_ref[...]
        row = w_ref[pl.ds(oq, 128), :]
        g = dot6(wide_left(wd), tall_right(row))
        inside = (lane_all >= oq) & (lane_all < oq + 128)
        done = jnp.where(lane_all < oq, g, 0.0)
        w_ref[pl.ds(oq, 128), :] = done if last else jnp.where(p > 0, done, row)
        l_ref[pl.ds(oq, 128), pl.ds(oq, 128)] = u_ref[...].T
        if last:
            w_ref[pl.ds(oq, 128), pl.ds(oq, 128)] = wd
            wh[pl.ds(oq, 128), :], wl[pl.ds(oq, 128), :] = halves(w_ref[pl.ds(oq, 128), :])
            return
        g_ref[...] = g
        g_ref[:, pl.ds(oq, 128)] += wd
        right = tall_right(g_ref[...])
        for i in range(1, nb):
            li = jnp.where(q < i, g[:, i * 128:(i + 1) * 128], 0.0).T
            l_ref[i * 128:(i + 1) * 128, pl.ds(oq, 128)] = jnp.where(q < i, li, l_ref[i * 128:(i + 1) * 128, pl.ds(oq, 128)])
            w_ref[i * 128:(i + 1) * 128, :] -= dot6(wide_left(li), right)
        w_ref[pl.ds(oq, 128), pl.ds(oq, 128)] = jnp.where(p > 0, wd, w_ref[pl.ds(oq, 128), pl.ds(oq, 128)])
        wh[pl.ds(oq, 128), :], wl[pl.ds(oq, 128), :] = halves(done)
        wh[pl.ds(oq, 128), pl.ds(oq, 128)], wl[pl.ds(oq, 128), pl.ds(oq, 128)] = halves(wd)

    def panel(p, carry):
        o = pl.multiple_of(p * 128, 128)
        o1 = pl.multiple_of(jnp.minimum(p + 1, nb - 1) * 128, 128)
        s = [d_ref[8 * g:8 * g + 8, :] for g in range(16)]
        t = [(lane == sub + 8 * g).astype(jnp.float32) for g in range(16)]
        s, t = factor_tile(s, t)
        settle(p, False)
        for g in range(16):
            u_ref[8 * g:8 * g + 8, :] = jnp.where(lane >= sub + 8 * g, s[g], 0.0)
            wd_ref[8 * g:8 * g + 8, :] = t[g]
        un = dot6(wide_left(wd_ref[...]), tall_right(w_ref[pl.ds(o, 128), pl.ds(o1, 128)]))
        d_ref[...] = w_ref[pl.ds(o1, 128), pl.ds(o1, 128)] - dot6(wide_left(un.T), tall_right(un))
        for k in range(nb):
            @pl.when(p == k)
            def _():
                transfers(exchange, k + 1)
        return carry
    lax.fori_loop(0, nb, panel, 0)
    keep_own.wait()

    def fetch(b, slot):
        rows = rows_ref.at[pl.ds(pl.multiple_of(b * GROUP, GROUP), GROUP)]
        return pltpu.make_async_copy(rows, r_buf.at[slot], sem_in.at[slot])

    def store(b, slot):
        part = pl.ds(pl.multiple_of(b * GROUP, GROUP), GROUP)
        return (pltpu.make_async_copy(yh_buf.at[slot], yh_ref.at[part], sem_out.at[slot, 0]),
                pltpu.make_async_copy(yl_buf.at[slot], yl_ref.at[part], sem_out.at[slot, 1]))

    blocks = rows_ref.shape[0] // GROUP
    fetch(0, 0).start()
    settle(nb, True)
    save_l = pltpu.make_async_copy(l_ref, l_out, sem_l)
    save_l.start()

    def passing(b, j):
        for k in range(blocks):
            at = nb + 1 + STEPS * k + j
            if at in RELAYS.values():
                @pl.when(b == k)
                def _():
                    transfers(exchange, at)

    def transform(b, carry):
        slot = lax.rem(b, 2)
        fetch(b, slot).wait()

        @pl.when(b + 1 < blocks)
        def _():
            fetch(b + 1, 1 - slot).start()

        @pl.when(b >= 2)
        def _():
            for copy in store(b - 2, slot):
                copy.wait()
        rh[...], rl[...] = halves(r_buf[slot])
        for j, p in enumerate(range(0, n, BLOCK)):
            e = p + BLOCK
            z = dot3((rh[:, :e], rl[:, :e]), (wh[p:e, :e], wl[p:e, :e]), NT)
            zf[:, p:e] = z
            yh_buf[slot, :, p:e], yl_buf[slot, :, p:e] = halves(z)
            passing(b, j)
        for copy in store(b, slot):
            copy.start()
        per = GROUP // own_ref.shape[0]

        @pl.when(me // per == b)
        def _():
            x_ref[...] = zf[pl.ds(pl.multiple_of(lax.rem(me, per) * own_ref.shape[0], own_ref.shape[0]), own_ref.shape[0]), :]
        return carry
    lax.fori_loop(0, blocks, transform, 0)
    late = sorted({at for (h, a, b, hop), at in RELAYS.items() if (a, b) == (2, 2) and at >= nb + 1 + STEPS * blocks})
    for point in range(nb + 1 + STEPS * blocks, len(POINTS)):
        transfers(exchange, point, near=True)
    saves = []
    size = cols_ref.shape[0] // 2

    def column_factor(early):
        exchange.finish_cols(early)
        half = exchange.early_half() if early else 1 - exchange.early_half()
        part = pl.ds(pl.multiple_of(half * size, size), size)
        ch[...], cl[...] = halves(cols_ref[part, :])
        for j, p in enumerate(range(0, n, BLOCK)):
            e = p + BLOCK
            z = dot3((ch[:, :e], cl[:, :e]), (wh[p:e, :e], wl[p:e, :e]), NT)
            zh_buf[part, p:e], zl_buf[part, p:e] = halves(z)
            for k, (a, b) in enumerate(((zh_buf, zh_ref), (zl_buf, zl_ref))):
                saves.append(pltpu.make_async_copy(a.at[part, p:e], b.at[part, p:e], sem_z.at[int(early), j, k]))
                saves[-1].start()
            if early and j % 2 == 1 and late:
                transfers(exchange, late.pop(0), far=True)
    column_factor(True)
    for point in late:
        transfers(exchange, point, far=True)
    column_factor(False)
    exchange.finish()
    for b in (blocks - 2, blocks - 1):
        for copy in store(b, b % 2):
            copy.wait()
    for copy in [save_l] + saves:
        copy.wait()


def factor(front_diag, own, cols):
    f32, bf = jnp.float32, jnp.bfloat16
    n = front_diag.shape[0]
    rows = lax.axis_size("col") * own.shape[0]
    vm, anywhere = pl.BlockSpec(memory_space=pltpu.VMEM), pl.BlockSpec(memory_space=pl.ANY)
    hbm = pl.BlockSpec(memory_space=pl.ANY)
    dma = pltpu.SemaphoreType.DMA
    return pl.pallas_call(
        factor_kernel,
        out_shape=(
            jax.ShapeDtypeStruct((n, n), f32),
            jax.ShapeDtypeStruct(own.shape, f32),
            jax.ShapeDtypeStruct((rows, n), bf),
            jax.ShapeDtypeStruct((rows, n), bf),
            jax.ShapeDtypeStruct((cols, n), bf),
            jax.ShapeDtypeStruct((cols, n), bf),
            jax.ShapeDtypeStruct((rows, n), f32),
        ),
        in_specs=[hbm, hbm],
        out_specs=(anywhere, vm, hbm, hbm, anywhere, anywhere, hbm),
        scratch_shapes=[
            pltpu.VMEM((n, n), f32), pltpu.VMEM((n, n), f32), pltpu.VMEM((128, n), f32),
            pltpu.VMEM((128, 128), f32), pltpu.VMEM((128, 128), f32), pltpu.VMEM((128, 128), f32),
            pltpu.VMEM((cols, n), f32),
            pltpu.VMEM((n, n), bf), pltpu.VMEM((n, n), bf),
            pltpu.VMEM((2, GROUP, n), f32), pltpu.VMEM((GROUP, n), f32),
            pltpu.VMEM((GROUP, n), bf), pltpu.VMEM((GROUP, n), bf),
            pltpu.VMEM((2, GROUP, n), bf), pltpu.VMEM((2, GROUP, n), bf),
            pltpu.VMEM((cols // 2, n), bf), pltpu.VMEM((cols // 2, n), bf),
            pltpu.VMEM((cols, n), bf), pltpu.VMEM((cols, n), bf),
            pltpu.VMEM(own.shape, f32),
            dma, dma, dma, dma((2,)), dma((2, 2)), dma((2, n // BLOCK, 2)),
            dma((64,)), dma((64,)), dma((32,)), dma((32,)), dma((32,)), dma((32,)),
        ],
        compiler_params=pltpu.CompilerParams(vmem_limit_bytes=56 << 20, collective_id=0, has_side_effects=True),
        name="factor",
    )(front_diag, own)


UNIT = 2
AHEAD = 2


def update_kernel(pattern_ref, yh_ref, yl_ref, zh_ref, zl_ref, t_ref, l_ref, x_ref, o_ref, lo_ref, xo_ref,
                  yh, yl, zh, zl, t, l, x, sem_z, sem_in, sem_out, sem_l):
    n = t.shape[1]
    size = UNIT * BLOCK
    steps, cols = t.shape[0] // size, n // BLOCK
    first_row = lax.axis_index("row") * (steps * UNIT)
    first_col = lax.axis_index("col") * cols

    def keep(r, c):
        return (pattern_ref[c, r] != 0) & (first_row + r >= first_col + c)

    def inputs(i):
        part = slice(i * size, (i + 1) * size)
        return [pltpu.make_async_copy(a.at[part], b.at[part], sem_in.at[i, k])
                for k, (a, b) in enumerate(((yh_ref, yh), (yl_ref, yl), (t_ref, t)))]
    factors = [pltpu.make_async_copy(zh_ref, zh, sem_z.at[0]), pltpu.make_async_copy(zl_ref, zl, sem_z.at[1])]
    bands = l.shape[0] // BLOCK
    lower = [(slice(q * BLOCK, (q + 1) * BLOCK), slice(0, (q + 1) * BLOCK)) for q in range(bands)]
    passed = [pltpu.make_async_copy(l_ref.at[at], l.at[at], sem_l.at[q]) for q, at in enumerate(lower)]
    passed.append(pltpu.make_async_copy(x_ref, x, sem_l.at[bands]))
    passed_on = [pltpu.make_async_copy(l, lo_ref, sem_l.at[bands + 1]), pltpu.make_async_copy(x, xo_ref, sem_l.at[bands + 2])]
    outputs = []
    for copy in factors:
        copy.start()
    for copy in inputs(0):
        copy.start()
    for q in range(bands - 1):
        l[q * BLOCK:(q + 1) * BLOCK, (q + 1) * BLOCK:] = jnp.zeros((BLOCK, l.shape[1] - (q + 1) * BLOCK), jnp.float32)
    for copy in factors:
        copy.wait()
    for i in range(1, AHEAD):
        for copy in inputs(i):
            copy.start()
    for i in range(steps):
        for copy in inputs(i):
            copy.wait()
        if i + AHEAD < steps:
            for copy in inputs(i + AHEAD):
                copy.start()
        if i + AHEAD == steps:
            for copy in passed:
                copy.start()
        kept = [keep(i * UNIT + k // cols, k % cols) for k in range(UNIT * cols)]
        many = sum(k.astype(jnp.int32) for k in kept) > UNIT * cols // 2

        @pl.when(many)
        def _():
            rows = slice(i * size, (i + 1) * size)
            for j in range(cols):
                part = slice(j * BLOCK, (j + 1) * BLOCK)
                d = dot3((yh[rows, :], yl[rows, :]), (zh[part, :], zl[part, :]), NT)
                for r in range(UNIT):
                    at = slice(i * size + r * BLOCK, i * size + (r + 1) * BLOCK)
                    t[at, part] -= jnp.where(kept[r * cols + j], d[r * BLOCK:(r + 1) * BLOCK], 0.0)

        @pl.when(jnp.logical_not(many))
        def _():
            def block(k, carry):
                rows = pl.ds(pl.multiple_of(i * size + k // cols * BLOCK, BLOCK), BLOCK)
                part = pl.ds(pl.multiple_of(k % cols * BLOCK, BLOCK), BLOCK)

                @pl.when(keep(i * UNIT + k // cols, k % cols))
                def _():
                    t[rows, part] -= dot3((yh[rows, :], yl[rows, :]), (zh[part, :], zl[part, :]), NT)
                return carry
            lax.fori_loop(0, UNIT * cols, block, 0)
        rows = slice(i * size, (i + 1) * size)
        outputs.append(pltpu.make_async_copy(t.at[rows], o_ref.at[rows], sem_out.at[i]))
        outputs[-1].start()
        if i == steps - 2:
            for copy in passed:
                copy.wait()
            for copy in passed_on:
                copy.start()
    for copy in outputs + passed_on:
        copy.wait()


def update(pattern, yh, yl, zh, zl, trailing, diag_factor, panel_factor):
    f32, bf = jnp.float32, jnp.bfloat16
    m, n = trailing.shape
    steps = m // (UNIT * BLOCK)
    anywhere, hbm = pl.BlockSpec(memory_space=pl.ANY), pl.BlockSpec(memory_space=pl.ANY)
    dma = pltpu.SemaphoreType.DMA
    return pl.pallas_call(
        update_kernel,
        out_shape=(jax.ShapeDtypeStruct((m, n), f32), jax.ShapeDtypeStruct(diag_factor.shape, f32),
                   jax.ShapeDtypeStruct(panel_factor.shape, f32)),
        in_specs=[pl.BlockSpec(memory_space=pltpu.SMEM), hbm, hbm, anywhere, anywhere, hbm, anywhere, anywhere],
        out_specs=(hbm,) * 3,
        scratch_shapes=[
            pltpu.VMEM(yh.shape, bf), pltpu.VMEM(yl.shape, bf), pltpu.VMEM(zh.shape, bf), pltpu.VMEM(zl.shape, bf),
            pltpu.VMEM((m, n), f32), pltpu.VMEM(diag_factor.shape, f32), pltpu.VMEM(panel_factor.shape, f32),
            dma((2,)), dma((steps, 3)), dma((steps,)), dma((diag_factor.shape[0] // BLOCK + 3,)),
        ],
        compiler_params=pltpu.CompilerParams(vmem_limit_bytes=60 << 20),
        name="update",
    )(pattern, yh, yl, zh, zl, trailing, diag_factor, panel_factor)


def local(front_diag, panel_rows, trailing, pattern):
    diag_factor, panel_factor, yh, yl, zh, zl, _ = factor(front_diag, panel_rows, trailing.shape[1])
    schur, diag_factor, panel_factor = update(pattern.T, yh, yl, zh, zl, trailing, diag_factor, panel_factor)
    return (diag_factor, panel_factor, schur)


def solution(mesh):
    return jax.shard_map(
        local,
        mesh=mesh,
        in_specs=(P(), P(("row", "col"), None), P("row", "col"), P("row", "col")),
        out_specs=(P(), P(("row", "col"), None), P("row", "col")),
        check_vma=False,
    )
```
